256 devices in a mesh: src: 32 (over y_hi, z, core), tgt: 8 (over x, y_lo).
Axes of the slice: x: 4, y: 4 (y_hi: 2, y_lo: 2; y = y_hi * 2 + y_lo), z: 8, core: 2. Of those that a mesh axis runs over, the one named last changes fastest.
Arguments:
- edge_states: bfloat16 [32, 8, 512, 1024], P('src', 'tgt'), may hold values from -6 to 6
- triplet_coeff: bfloat16 [32, 8, 16, 128, 128], P('src', 'tgt'), may hold values from -0.3984375 to 0.3984375
- block_target: int32 [32, 8, 16], P('src', 'tgt'), may hold values from 0 to 3
- block_source: int32 [32, 8, 16], P('src', 'tgt'), may hold values from 0 to 127
- block_count: int32 [32, 8], P('src', 'tgt'), may hold values from 2 to 16, as said below
- reverse_slot: int32 [32, 8, 512], P('src', 'tgt'), may hold values from 0 to 511, as said below
- w_proj: bfloat16 [2, 1024, 64], replicated, may hold values from -0.1875 to 0.1875
- w_up: bfloat16 [2, 64, 1024], replicated, may hold values from -0.75 to 0.75
- w_in: bfloat16 [2, 1024, 1024], replicated, may hold values from -0.1875 to 0.1875
- w_out: bfloat16 [2, 1024, 1024], replicated, may hold values from -0.1875 to 0.1875
- norm_gain: float32 [2, 1024], replicated, may hold values from 0.5 to 2
Outputs:
- edge_final: bfloat16 [32, 8, 512, 1024], P('src', 'tgt')
The draws below stay inside these ranges and needn't reach their ends.
Inputs may be any that keep to these rules, and one draw needn't show every extreme that they name: `block_count`: each tile uses between 2 and 16 blocks; some tile uses all 16 in every draw. Reverse edges pair up: with C = 4, for tile (p, q) with p = a * C + r and its mirror tile (q * C + r, a), the two reverse_slot rows are inverse permutations of 0 to 511; on a tile with a = q the row is a permutation that is its own inverse without fixed points.
All inputs are finite; a program needn't handle non-finite values.
Results may differ from the reference program's by a relative error of at most 0.014.
Values may be sent and summed in bfloat16 or wider, within the bound.
A program may use at most 64 MiB of HBM per device.

```python
import math
import jax
import jax.numpy as jnp
from jax import lax

D = 1024
TRIP = 64
E_TILE = 512
BLK = 128
LAYERS = 2
NB = 16
N_SRC = 32
N_TGT = 8


def draw_block_count(key, part):
    key_base = jax.random.fold_in(key, 11)
    key_full = jax.random.fold_in(key, 12)
    key_pick = jax.random.fold_in(key, 13)
    lowest = max(1, NB // 8)
    base_counts = jax.random.randint(key_base, (N_SRC, N_TGT), lowest, NB // 2 + 1)
    full_tiles = jax.random.randint(key_full, (N_SRC, N_TGT), 0, 16) == 0
    counts = jnp.where(full_tiles, NB, base_counts).reshape(-1)
    chosen = jax.random.randint(key_pick, (), 0, N_SRC * N_TGT)
    counts = jnp.where(jnp.arange(N_SRC * N_TGT) == chosen, NB, counts)
    return counts.reshape(N_SRC, N_TGT).astype(jnp.int32)


def draw_reverse_slot(key, part):
    groups = N_TGT
    copies = N_SRC // groups
    tile_keys = jax.random.split(jax.random.fold_in(key, 21), copies * groups * groups)
    perms = jax.vmap(lambda single: jax.random.permutation(single, E_TILE))(tile_keys)
    perms = perms.reshape(copies, groups, groups, E_TILE).astype(jnp.int32)
    inverse = jnp.argsort(perms, axis=-1).astype(jnp.int32)
    partner = perms.reshape(copies, groups, groups, E_TILE // 2, 2)[..., ::-1].reshape(copies, groups, groups, E_TILE)
    involution = jnp.take_along_axis(partner, inverse, axis=-1)
    row_group = jnp.arange(groups)[None, :, None, None]
    col_group = jnp.arange(groups)[None, None, :, None]
    result = jnp.where(row_group < col_group, perms, jnp.where(row_group > col_group, inverse.swapaxes(1, 2), involution))
    result = result.transpose(1, 0, 2, 3)
    return result.reshape(N_SRC, N_TGT, E_TILE).astype(jnp.int32)


def touch_ends(values, stream_key, smallest, high):
    extent = values.shape
    spot = [jax.random.randint(jax.random.fold_in(stream_key, axis), (), 0, extent[axis]) for axis in range(len(extent))]
    values = values.at[tuple(spot)].set(smallest)
    longest = extent.index(max(extent))
    spot[longest] = (spot[longest] + 1) % extent[longest]
    return values.at[tuple(spot)].set(high)


def block_levels(rng, extent, cuts, smallest, largest):
    loudness = 1.0
    for position, blocks in cuts:
        draws = jax.random.uniform(jax.random.fold_in(jax.random.fold_in(rng, 6), position), (blocks,), jnp.float32, smallest / len(cuts), largest / len(cuts))
        loudness = loudness * jnp.repeat(jnp.exp(draws), extent[position] // blocks).reshape((-1,) + (1,) * (len(extent) - 1 - position))
    return loudness


def gaussian(rng, extent, width, bound, cuts=(), dtype=jnp.bfloat16):
    level = block_levels(rng, extent, cuts, -0.22, 0.18) if cuts else 1.0
    array = jax.random.normal(rng, extent, jnp.float32) * width * level
    return jnp.minimum(jnp.maximum(array, -bound), bound).astype(dtype)


def setup_inputs(seed: int = 0) -> dict:
    seeds = jax.random.split(jax.random.key(seed), 12)
    edge_states = gaussian(seeds[0], (N_SRC, N_TGT, E_TILE, D), 1.0, 6.0, ((0, 32), (1, 8)))
    triplet_coeff = gaussian(seeds[1], (N_SRC, N_TGT, NB, BLK, BLK), 0.05, 0.3984375, ((0, 32), (1, 8)))
    block_target = touch_ends(jax.random.randint(seeds[2], (N_SRC, N_TGT, NB), 0, E_TILE // BLK), jax.random.fold_in(seeds[2], 1), 0, (E_TILE // BLK) - 1).astype(jnp.int32)
    block_source = touch_ends(jax.random.randint(seeds[3], (N_SRC, N_TGT, NB), 0, N_SRC * E_TILE // BLK), jax.random.fold_in(seeds[3], 1), 0, (N_SRC * E_TILE // BLK) - 1).astype(jnp.int32)
    block_count = draw_block_count(jax.random.fold_in(seeds[11], 71), 0)
    reverse_slot = draw_reverse_slot(jax.random.fold_in(seeds[11], 71), 0)
    w_proj = gaussian(seeds[6], (LAYERS, D, TRIP), D ** -0.5, 0.1875)
    w_up = gaussian(seeds[7], (LAYERS, TRIP, D), TRIP ** -0.5, 0.75)
    w_in = gaussian(seeds[8], (LAYERS, D, D), D ** -0.5, 0.1875)
    w_out = gaussian(seeds[9], (LAYERS, D, D), D ** -0.5, 0.1875)
    norm_gain = jnp.clip(jnp.exp(jax.random.uniform(seeds[10], (LAYERS, D), jnp.float32, math.log(0.5), math.log(2.0))), 0.5, 2.0)
    return dict(edge_states=edge_states, triplet_coeff=triplet_coeff, block_target=block_target, block_source=block_source, block_count=block_count, reverse_slot=reverse_slot, w_proj=w_proj, w_up=w_up, w_in=w_in, w_out=w_out, norm_gain=norm_gain)


def mirror_of(values, reverse_slot):
    groups = N_TGT
    copies = N_SRC // groups
    turned = values.reshape((groups, copies, groups) + values.shape[2:]).swapaxes(0, 2).reshape(values.shape)
    return jnp.take_along_axis(turned, reverse_slot[..., None], axis=2)

def reference(edge_states, triplet_coeff, block_target, block_source, block_count, reverse_slot, w_proj, w_up, w_in, w_out, norm_gain):
    out_blocks = E_TILE // BLK
    live_mask = (jnp.arange(NB)[None, None, :] < block_count[:, :, None]).astype(jnp.float32)
    placing = (block_target[..., None] == jnp.arange(out_blocks)[None, None, None, :]).astype(jnp.float32) * live_mask[..., None]
    coeffs = triplet_coeff.astype(jnp.float32)
    state = edge_states
    for layer_index in range(LAYERS):
        proj = jnp.einsum('sted,dc->stec', state.astype(jnp.float32), w_proj[layer_index].astype(jnp.float32)).astype(jnp.bfloat16)
        pooled = proj.swapaxes(0, 1).reshape(N_TGT, N_SRC * out_blocks, BLK, TRIP)
        picked = pooled[jnp.arange(N_TGT)[None, :, None], block_source]
        products = jnp.einsum('stbji,stbjc->stbic', coeffs, picked.astype(jnp.float32))
        agg = jnp.einsum('stbic,stbo->stoic', products, placing).reshape(N_SRC, N_TGT, E_TILE, TRIP).astype(jnp.bfloat16)
        summed = state.astype(jnp.float32) + jnp.einsum('stec,cd->sted', agg.astype(jnp.float32), w_up[layer_index].astype(jnp.float32))
        scale_inv = lax.rsqrt(lax.optimization_barrier(jnp.mean(summed * summed, axis=-1, keepdims=True)) + 1e-06)
        normed = (norm_gain[layer_index] * summed * scale_inv).astype(jnp.bfloat16)
        activated = jax.nn.silu(jnp.einsum('sted,dh->steh', normed.astype(jnp.float32), w_in[layer_index].astype(jnp.float32))).astype(jnp.bfloat16)
        branch = jnp.einsum('steh,hd->sted', activated.astype(jnp.float32), w_out[layer_index].astype(jnp.float32)).astype(jnp.bfloat16)
        state = (summed + branch.astype(jnp.float32) + mirror_of(branch, reverse_slot).astype(jnp.float32)).astype(jnp.bfloat16)
    return state
```

```python
import functools

import jax
import jax.numpy as jnp
from jax import lax
from jax.experimental import pallas as pl
from jax.experimental.pallas import tpu as pltpu
from jax.sharding import PartitionSpec as P

MESH = pl.DeviceIdType.MESH
BF16 = jnp.bfloat16
F32 = jnp.float32
D = 1024
E = 512
T = 64
BLK = 128
NB = 16
SUB = 2
NBLK = 128


def place():
    s = lax.axis_index("src")
    t = lax.axis_index("tgt")
    return dict(y1=s // 16, z=(s // 2) % 8, c=s % 2, x=t // 2, y0=t % 2)


def device(x, y1, y0, z, c):
    return (y1 * 16 + z * 2 + c, x * 2 + y0)


def kernel(
    tgt_s, src_s, cnt_s, st_h, coef_h, rs_ref, wp_h, wup_h, win_h, wout_h, gain_ref, out_ref,
    st, coef, wp, wup, win, wout, g0, g1, l1, l2, fin, perm, lhs, aggt, aggm, pbt, pbm,
    summed, branch, mst, msum, mbr, nrm, act, lsem,
    gs, yr, zr, sr, l1s, l1r, l2s, l2r, l3s, l3r, ms, mr,
):
    k = place()
    x, y1, y0, z, c = k["x"], k["y1"], k["y0"], k["z"], k["c"]
    z2, z1, z0 = z // 4, (z // 2) % 2, z % 2
    x1, x0 = x // 2, x % 2
    me_slot = y1 * 16 + z * 2 + c

    sib = device(x, y1, y0, z, 1 - c)
    ypart = device(x, 1 - y1, y0, z, c)
    zup = device(x, y1, y0, (z + 1) % 8, c)
    zdn = device(x, y1, y0, (z + 7) % 8, c)
    mirror = device(y1 * 2 + z2, x1, z1, x0 * 4 + y0 * 2 + z0, c)
    diag = (x1 == y1) & (x0 == z2) & (y0 == z1)
    not_diag = jnp.logical_not(diag)

    def leg2(s):
        s1, s0 = s // 2, s % 2
        dest = device(x, s1, z1, s0 * 4 + y0 * 2 + z0, c)
        own = (y1 == s1) & (y0 == z1) & (z2 == s0)
        return dest, own

    xs = [(x + i) % 4 for i in range(1, 4)]

    bar = pltpu.get_barrier_semaphore()

    def signal(d):
        pl.semaphore_signal(bar, inc=1, device_id=d, device_id_type=MESH)

    @pl.when(not_diag)
    def _():
        signal(mirror)

    for s in range(4):
        dest, own = leg2(s)

        @pl.when(jnp.logical_not(own))
        def _(dest=dest):
            signal(dest)

    for d in (ypart, zup, zdn, sib):
        signal(d)
    for xx in xs:
        signal(device(xx, y1, y0, z, c))

    loads = [
        pltpu.make_async_copy(a, b, lsem.at[i])
        for i, (a, b) in enumerate(
            [(st_h, st), (wp_h, wp), (coef_h, coef), (wup_h, wup), (win_h.at[0], win.at[0]),
             (wout_h.at[0], wout.at[0]), (win_h.at[1], win.at[1]), (wout_h.at[1], wout.at[1])]
        )
    ]
    for cp in loads:
        cp.start()

    loads[0].wait()
    loads[1].wait()

    def proj_t(l, rows):
        return lax.dot_general(
            wp[l], rows, (((1,), (1,)), ((), ())), preferred_element_type=F32
        )

    def put_own(g, val):
        for b in range(4):
            g[me_slot * 4 + b] = val[:, b * BLK : (b + 1) * BLK].astype(BF16)

    put_own(g0, proj_t(0, st[...]))

    n_own2 = (y0 == z1).astype(jnp.int32)
    pl.semaphore_wait(bar, 4 + 3 + 4 - n_own2 + not_diag.astype(jnp.int32))

    def remote(src, dst, ss, rs, d):
        return pltpu.make_async_remote_copy(
            src_ref=src, dst_ref=dst, send_sem=ss, recv_sem=rs, device_id=d, device_id_type=MESH
        )

    def make_gather(l, g):
        def piece(col, zz, lo=0, n=4):
            return g.at[pl.ds((col * 16 + zz * 2 + c) * 4 + lo, n)]

        def to_sib(p):
            remote(p, p, gs.at[l], sr.at[l], sib).start()

        def z_copy(p, direction, dist, b):
            return remote(
                p, p, gs.at[l], zr.at[l, direction, dist - 1, b], zup if direction == 0 else zdn
            )

        def part(direction, dist, b, at_dist):
            col = y1 if b == 0 else 1 - y1
            zz = (z + 8 - at_dist) % 8 if direction == 0 else (z + at_dist) % 8
            if dist == 4:
                return piece(col, zz, 0 if direction == 0 else 2, 2)
            return piece(col, zz)

        def start():
            own = piece(y1, z)
            for direction in (0, 1):
                z_copy(part(direction, 1, 0, 0), direction, 1, 0).start()
            remote(own, own, gs.at[l], yr.at[l], ypart).start()
            to_sib(own)

        def from_y():
            other = piece(1 - y1, z)
            remote(other, other, gs.at[l], yr.at[l], ypart).wait_recv()
            for direction in (0, 1):
                z_copy(part(direction, 1, 1, 0), direction, 1, 1).start()
            to_sib(other)

        def step(dist, b):
            for direction in (0, 1):
                got = part(direction, dist, b, dist)
                z_copy(got, direction, dist, b).wait_recv()
                if dist < 4:
                    z_copy(part(direction, dist + 1, b, dist), direction, dist + 1, b).start()
                to_sib(got)

        def finish():
            half = g.at[pl.ds(0, 64)]
            remote(half, half, gs.at[l], sr.at[l], sib).wait_recv()

        def drain():
            a = g.at[pl.ds(0, 4 * 31)]
            remote(a, a, gs.at[l], sr.at[l], sib).wait_send()

        return start, from_y, step, finish, drain

    gat0 = make_gather(0, g0)
    gat1 = make_gather(1, g1)
    gat0[0]()

    rows_sub = BLK // SUB

    def sub(ref, slot, j):
        return ref.at[slot, pl.ds(j * rows_sub, rows_sub)]

    def st_sub(chunk, j):
        return st.at[pl.ds(chunk * BLK + j * rows_sub, rows_sub)]

    def leg1_start(j):
        for i, xx in enumerate(xs):
            remote(
                st_sub(xx, j), sub(l1, x, j), l1s.at[j], l1r.at[j, 3 - 1 - i], device(xx, y1, y0, z, c)
            ).start()
        pltpu.make_async_copy(st_sub(x, j), sub(l1, x, j), l1r.at[j, 3]).start()

    def leg1_wait(j):
        for i, xx in enumerate(xs):
            remote(st_sub(xx, j), sub(l1, xx, j), l1s.at[j], l1r.at[j, i], sib).wait_recv()
        pltpu.make_async_copy(st_sub(x, j), sub(l1, x, j), l1r.at[j, 3]).wait()

    def leg2_start(j):
        for s in range(4):
            dest, own = leg2(s)
            there = y1 * 2 + z2

            @pl.when(jnp.logical_not(own))
            def _(dest=dest, s=s):
                remote(
                    sub(l1, s, j), sub(l2, there, j), l2s.at[j], l2r.at[j, there], dest
                ).start()

            @pl.when(own)
            def _(s=s):
                pltpu.make_async_copy(sub(l1, s, j), sub(l2, s, j), l2r.at[j, s]).start()

    def leg2_wait(j):
        for s in range(4):
            dest, own = leg2(s)

            @pl.when(jnp.logical_not(own))
            def _(s=s, dest=dest):
                remote(sub(l1, s, j), sub(l2, s, j), l2s.at[j], l2r.at[j, s], dest).wait_recv()

            @pl.when(own)
            def _(s=s):
                pltpu.make_async_copy(sub(l1, s, j), sub(l2, s, j), l2r.at[j, s]).wait()

    def fin_sub(chunk, j):
        return fin.at[pl.ds(chunk * BLK + j * rows_sub, rows_sub)]

    def leg3_start(j):
        for i, xx in enumerate(xs):
            remote(
                sub(l2, xx, j), fin_sub(x, j), l3s.at[j], l3r.at[j, 3 - 1 - i], device(xx, y1, y0, z, c)
            ).start()
        pltpu.make_async_copy(sub(l2, x, j), fin_sub(x, j), l3r.at[j, 3]).start()

    def leg3_wait(j):
        for i, xx in enumerate(xs):
            remote(sub(l2, xx, j), fin_sub(xx, j), l3s.at[j], l3r.at[j, i], sib).wait_recv()
        pltpu.make_async_copy(sub(l2, x, j), fin_sub(x, j), l3r.at[j, 3]).wait()

    def legs_drain():
        for j in range(SUB):
            rows = pl.ds(0, rows_sub)
            three, four = l1.at[pl.ds(0, 3), rows], l1.at[pl.ds(0, 4), rows]
            remote(three, three, l1s.at[j], l1r.at[j, 0], sib).wait_send()
            remote(three, three, l3s.at[j], l3r.at[j, 0], sib).wait_send()

            @pl.when(y0 == z1)
            def _(j=j, three=three):
                remote(three, three, l2s.at[j], l2r.at[j, 0], sib).wait_send()

            @pl.when(y0 != z1)
            def _(j=j, four=four):
                remote(four, four, l2s.at[j], l2r.at[j, 0], sib).wait_send()

    def swap_start(i, src, dst):
        @pl.when(not_diag)
        def _():
            remote(src, dst, ms.at[i], mr.at[i], mirror).start()

        @pl.when(diag)
        def _():
            pltpu.make_async_copy(src, dst, mr.at[i]).start()

    def swap_wait(i, src, dst):
        @pl.when(not_diag)
        def _():
            remote(src, dst, ms.at[i], mr.at[i], mirror).wait_recv()

        @pl.when(diag)
        def _():
            pltpu.make_async_copy(src, dst, mr.at[i]).wait()

    def swap_drain(i, src, dst):
        @pl.when(not_diag)
        def _():
            remote(src, dst, ms.at[i], mr.at[i], mirror).wait_send()

    def triplets(g, out):
        live = cnt_s[0]
        zero = jnp.zeros((T, BLK), BF16)
        for b in range(NB):
            blk = g[src_s[b]]
            tb = jnp.where(b < live, tgt_s[b], -1)
            for o in range(4):
                lhs[o * T : (o + 1) * T, b * BLK : (b + 1) * BLK] = jnp.where(tb == o, blk, zero)
        acc = jnp.dot(lhs[...], coef[...].reshape(NB * BLK, BLK), preferred_element_type=F32)
        for o in range(4):
            out[:, o * BLK : (o + 1) * BLK] = acc[o * T : (o + 1) * T].astype(BF16)

    def permute_t(val):
        return jnp.dot(val, perm[...], preferred_element_type=F32)

    def norm(l, rows_ref, agg, sum_ref):
        def body(r, _):
            rows = pl.ds(pl.multiple_of(r * BLK, BLK), BLK)
            up = lax.dot_general(
                agg[:, rows], wup[l], (((0,), (0,)), ((), ())), preferred_element_type=F32
            )
            s = rows_ref[rows, :].astype(F32) + up
            sum_ref[rows, :] = s
            scale = lax.rsqrt(jnp.mean(s * s, axis=-1, keepdims=True) + 1e-06)
            nrm[rows, :] = (gain_ref[l : l + 1, :] * s * scale).astype(BF16)
            return 0

        lax.fori_loop(0, 4, body, 0)

    def hidden(l):
        def body(n, _):
            cols = pl.ds(pl.multiple_of(n * 256, 256), 256)
            h = jnp.dot(nrm[...], win[l, :, cols], preferred_element_type=F32)
            act[:, cols] = (h / (1.0 + jnp.exp(-h))).astype(BF16)
            return 0

        lax.fori_loop(0, 4, body, 0)

    def outer(l, br):
        def body(n, _):
            cols = pl.ds(pl.multiple_of(n * 256, 256), 256)
            br[:, cols] = jnp.dot(
                act[...], wout[l, :, cols], preferred_element_type=F32
            ).astype(BF16)
            return 0

        lax.fori_loop(0, 4, body, 0)

    def by_rows(f):
        def body(r, _):
            f(pl.ds(pl.multiple_of(r * BLK, BLK), BLK))
            return 0

        lax.fori_loop(0, 4, body, 0)

    for j in range(SUB):
        leg1_start(j)

    def onehot(rows, r):
        ids = lax.broadcasted_iota(jnp.int32, (BLK, E), 0) + r * BLK
        perm[rows, :] = jnp.where(ids == rs_ref[0:1, :], 1.0, 0.0).astype(BF16)

    def onehot_body(r, _):
        onehot(pl.ds(pl.multiple_of(r * BLK, BLK), BLK), r)
        return 0

    lax.fori_loop(0, 4, onehot_body, 0)

    start, from_y, step, finish, drain0 = gat0
    step(1, 0)
    from_y()
    step(1, 1)
    step(2, 0)
    leg1_wait(0)
    step(2, 1)
    step(3, 0)
    leg2_start(0)
    step(3, 1)
    step(4, 0)
    step(4, 1)
    leg1_wait(1)
    leg2_start(1)
    finish()

    loads[2].wait()
    triplets(g0, aggt.at[0])
    swap_start(0, aggt.at[0], aggm.at[0])
    for i in (3, 4, 5):
        loads[i].wait()
    norm(0, st, aggt.at[0], summed)
    hidden(0)
    outer(0, branch)
    pbt[...] = proj_t(1, branch[...]).astype(BF16)
    swap_start(1, pbt, pbm)

    def part_sum(rows):
        nrm[rows, :] = (summed[rows, :] + branch[rows, :].astype(F32)).astype(BF16)

    by_rows(part_sum)
    half1 = proj_t(1, nrm[...])
    swap_wait(1, pbt, pbm)
    put_own(g1, half1 + permute_t(pbm[...]))
    start, from_y, step, finish, drain1 = gat1
    start()
    leg2_wait(0)
    leg3_start(0)
    step(1, 0)
    from_y()
    step(1, 1)
    step(2, 0)
    step(2, 1)
    step(3, 0)
    step(3, 1)
    step(4, 0)
    step(4, 1)
    leg2_wait(1)
    leg3_start(1)
    finish()
    triplets(g1, aggt.at[1])
    swap_start(2, aggt.at[1], aggm.at[1])

    swap_wait(0, aggt.at[0], aggm.at[0])
    act[0:T, 0:E] = permute_t(aggm[0]).astype(BF16)
    aggm[0] = act[0:T, 0:E]
    leg3_wait(0)
    leg3_wait(1)

    def take_rows(n, _):
        cols = pl.ds(pl.multiple_of(n * 256, 256), 256)
        mst[:, cols] = lax.dot_general(
            perm[...], fin[:, cols], (((0,), (0,)), ((), ())), preferred_element_type=F32
        ).astype(BF16)
        return 0

    lax.fori_loop(0, 4, take_rows, 0)
    norm(0, mst, aggm.at[0], msum)
    hidden(0)
    outer(0, mbr)

    def next_state(rows):
        b = branch[rows, :].astype(F32)
        m = mbr[rows, :].astype(F32)
        st[rows, :] = ((summed[rows, :] + b) + m).astype(BF16)
        mst[rows, :] = ((msum[rows, :] + m) + b).astype(BF16)

    legs_drain()
    by_rows(next_state)

    for i in (6, 7):
        loads[i].wait()
    norm(1, st, aggt.at[1], summed)
    hidden(1)
    outer(1, branch)
    swap_wait(2, aggt.at[1], aggm.at[1])
    act[0:T, 0:E] = permute_t(aggm[1]).astype(BF16)
    aggm[1] = act[0:T, 0:E]
    norm(1, mst, aggm.at[1], msum)
    hidden(1)
    outer(1, mbr)

    def final(rows):
        out_ref[rows, :] = (
            (summed[rows, :] + branch[rows, :].astype(F32)) + mbr[rows, :].astype(F32)
        ).astype(BF16)

    by_rows(final)

    drain0()
    drain1()
    swap_drain(0, aggt.at[0], aggm.at[0])
    swap_drain(1, pbt, pbm)
    swap_drain(2, aggt.at[1], aggm.at[1])


def local(
    edge_states, triplet_coeff, block_target, block_source, block_count, reverse_slot,
    w_proj, w_up, w_in, w_out, norm_gain,
):
    vmem = pl.BlockSpec(memory_space=pltpu.VMEM)
    smem = pl.BlockSpec(memory_space=pltpu.SMEM)
    hbm = pl.BlockSpec(memory_space=pl.ANY)
    dma = pltpu.SemaphoreType.DMA
    out = pl.pallas_call(
        kernel,
        out_shape=jax.ShapeDtypeStruct((E, D), BF16),
        in_specs=[smem, smem, smem, hbm, hbm, vmem, hbm, hbm, hbm, hbm, vmem],
        out_specs=vmem,
        scratch_shapes=[
            pltpu.VMEM((E, D), BF16),
            pltpu.VMEM((NB, BLK, BLK), BF16),
            pltpu.VMEM((2, T, D), BF16),
            pltpu.VMEM((2, T, D), BF16),
            pltpu.VMEM((2, D, D), BF16),
            pltpu.VMEM((2, D, D), BF16),
            pltpu.VMEM((NBLK, T, BLK), BF16),
            pltpu.VMEM((NBLK, T, BLK), BF16),
            pltpu.VMEM((4, BLK, D), BF16),
            pltpu.VMEM((4, BLK, D), BF16),
            pltpu.VMEM((E, D), BF16),
            pltpu.VMEM((E, E), BF16),
            pltpu.VMEM((4 * T, NB * BLK), BF16),
            pltpu.VMEM((2, T, E), BF16),
            pltpu.VMEM((2, T, E), BF16),
            pltpu.VMEM((T, E), BF16),
            pltpu.VMEM((T, E), BF16),
            pltpu.VMEM((E, D), F32),
            pltpu.VMEM((E, D), BF16),
            pltpu.VMEM((E, D), BF16),
            pltpu.VMEM((E, D), F32),
            pltpu.VMEM((E, D), BF16),
            pltpu.VMEM((E, D), BF16),
            pltpu.VMEM((E, D), BF16),
            dma((8,)),
            dma((2,)),
            dma((2,)),
            dma((2, 2, 4, 2)),
            dma((2,)),
            dma((SUB,)), dma((SUB, 4)),
            dma((SUB,)), dma((SUB, 4)),
            dma((SUB,)), dma((SUB, 4)),
            dma((3,)), dma((3,)),
        ],
        compiler_params=pltpu.CompilerParams(
            collective_id=0, has_side_effects=True, vmem_limit_bytes=60 << 20
        ),
        name="edge_layers",
    )(
        block_target[0, 0], block_source[0, 0], block_count[0], edge_states[0, 0],
        triplet_coeff[0, 0], reverse_slot[0], jnp.swapaxes(w_proj, 1, 2), w_up, w_in, w_out,
        norm_gain,
    )
    return out[None, None]


def solution(mesh):
    return jax.shard_map(
        local,
        mesh=mesh,
        in_specs=(
            P("src", "tgt", None, None),
            P("src", "tgt", None, None, None),
            P("src", "tgt", None),
            P("src", "tgt", None),
            P("src", "tgt"),
            P("src", "tgt", None),
            P(),
            P(),
            P(),
            P(),
            P(),
        ),
        out_specs=P("src", "tgt", None, None),
        check_vma=False,
    )
```

```python
import functools

import jax
import jax.numpy as jnp
from jax import lax
from jax.experimental import pallas as pl
from jax.experimental.pallas import tpu as pltpu
from jax.sharding import PartitionSpec as P

MESH = pl.DeviceIdType.MESH
BF16 = jnp.bfloat16
F32 = jnp.float32
D = 1024
E = 512
T = 64
BLK = 128
NB = 16
SUB = 4
ROWS = BLK // SUB
NBLK = 128


def place():
    s = lax.axis_index("src")
    t = lax.axis_index("tgt")
    return dict(y1=s // 16, z=(s // 2) % 8, c=s % 2, x=t // 2, y0=t % 2)


def device(x, y1, y0, z, c):
    return (y1 * 16 + z * 2 + c, x * 2 + y0)


def kernel(
    tgt_s, src_s, cnt_s, st_h, coef_h, rs_ref, wp_h, wup_h, win_h, wout_h, gain_ref, out_ref,
    st, coef, wp, wup, win, wout, g0, g1, l1, l2, rel, fin, perm, lhs, aggt, aggm, pbt, pbm,
    summed, branch, mst, msum, mbr, nrm, act, lsem,
    gs, yr, zr, sr, l1s, l1r, l2s, l2r, l2as, l2ar, l3s, l3r, ms, mr,
):
    k = place()
    x, y1, y0, z, c = k["x"], k["y1"], k["y0"], k["z"], k["c"]
    z2, z1, z0 = z // 4, (z // 2) % 2, z % 2
    x1, x0 = x // 2, x % 2
    me_slot = y1 * 16 + z * 2 + c

    sib = device(x, y1, y0, z, 1 - c)
    ypart = device(x, 1 - y1, y0, z, c)
    zup = device(x, y1, y0, (z + 1) % 8, c)
    zdn = device(x, y1, y0, (z + 7) % 8, c)
    mirror = device(y1 * 2 + z2, x1, z1, x0 * 4 + y0 * 2 + z0, c)
    diag = (x1 == y1) & (x0 == z2) & (y0 == z1)
    not_diag = jnp.logical_not(diag)

    def leg2(s):
        s1, s0 = s // 2, s % 2
        dest = device(x, s1, z1, s0 * 4 + y0 * 2 + z0, c)
        own = (y1 == s1) & (y0 == z1) & (z2 == s0)
        return dest, own

    xs = [(x + i) % 4 for i in range(1, 4)]

    bar = pltpu.get_barrier_semaphore()

    def signal(d):
        pl.semaphore_signal(bar, inc=1, device_id=d, device_id_type=MESH)

    @pl.when(not_diag)
    def _():
        signal(mirror)

    for s in range(4):
        dest, own = leg2(s)

        @pl.when(jnp.logical_not(own))
        def _(dest=dest):
            signal(dest)

    ys = [(y1 * 2 + y0 + i) % 4 for i in range(1, 4)]
    for yy in ys:
        signal(device(x, yy // 2, yy % 2, z, c))
    for i in (1, 2, 4, 6, 7):
        signal(device(x, y1, y0, (z + i) % 8, c))
    signal(sib)
    for xx in xs:
        signal(device(xx, y1, y0, z, c))

    loads = [
        pltpu.make_async_copy(a, b, lsem.at[i])
        for i, (a, b) in enumerate(
            [(st_h, st), (wp_h, wp), (coef_h, coef), (wup_h, wup), (win_h.at[0], win.at[0]),
             (wout_h.at[0], wout.at[0]), (win_h.at[1], win.at[1]), (wout_h.at[1], wout.at[1])]
        )
    ]
    for cp in loads:
        cp.start()

    loads[0].wait()
    loads[1].wait()

    def proj_t(l, rows):
        return lax.dot_general(
            wp[l], rows, (((1,), (1,)), ((), ())), preferred_element_type=F32
        )

    def put_own(g, val):
        for b in range(4):
            g[me_slot * 4 + b] = val[:, b * BLK : (b + 1) * BLK].astype(BF16)

    put_own(g0, proj_t(0, st[...]))

    n_own2 = (y0 == z1).astype(jnp.int32)
    pl.semaphore_wait(bar, 9 + 3 + 4 - n_own2 + not_diag.astype(jnp.int32))

    def remote(src, dst, ss, rs, d):
        return pltpu.make_async_remote_copy(
            src_ref=src, dst_ref=dst, send_sem=ss, recv_sem=rs, device_id=d, device_id_type=MESH
        )

    def make_gather(l, g):
        def half(col, zz, h):
            return g.at[pl.ds((col * 16 + zz * 2 + c) * 4 + 2 * h, 2)]

        def origin(direction, dist):
            return (z + 8 - dist) % 8 if direction == 0 else (z + dist) % 8

        def to_sib(p):
            remote(p, p, gs.at[l], sr.at[l], sib).start()

        def z_copy(p, direction, dist, h):
            return remote(
                p, p, gs.at[l], zr.at[l, direction, dist - 1, h], zup if direction == 0 else zdn
            )

        def y_copy(p, direction, dist, h):
            i = dist if direction == 0 or dist == 0 else 4 + dist
            return remote(p, p, gs.at[l], yr.at[l, i, h], ypart)

        def ways(dist, h):
            return (0, 1) if dist < 4 else (h,)

        def start():
            for h in (0, 1):
                own = half(y1, z, h)
                for direction in (0, 1):
                    z_copy(own, direction, 1, h).start()
                y_copy(own, 0, 0, h).start()
                to_sib(own)

        def z_step(dist, h):
            for direction in ways(dist, h):
                got = half(y1, origin(direction, dist), h)
                z_copy(got, direction, dist, h).wait_recv()
                if direction in ways(dist + 1, h) and dist < 4:
                    z_copy(got, direction, dist + 1, h).start()
                y_copy(got, direction, dist, h).start()
                to_sib(got)

        def y_step(dist, h):
            for direction in ways(dist, h) if dist else (0,):
                got = half(1 - y1, origin(direction, dist), h)
                y_copy(got, direction, dist, h).wait_recv()
                to_sib(got)

        def finish():
            all_sib = g.at[pl.ds(0, 64)]
            remote(all_sib, all_sib, gs.at[l], sr.at[l], sib).wait_recv()

        def drain():
            a = g.at[pl.ds(0, 4 * 31)]
            remote(a, a, gs.at[l], sr.at[l], sib).wait_send()

        return start, z_step, y_step, finish, drain

    gat0 = make_gather(0, g0)
    gat1 = make_gather(1, g1)
    gat0[0]()

    rows_sub = ROWS

    def sub(ref, slot, j):
        return ref.at[slot, pl.ds(j * rows_sub, rows_sub)]

    def st_sub(chunk, j):
        return st.at[pl.ds(chunk * BLK + j * rows_sub, rows_sub)]

    def leg1_start(j):
        for i, xx in enumerate(xs):
            remote(
                st_sub(xx, j), sub(l1, x, j), l1s.at[j], l1r.at[j, 3 - 1 - i], device(xx, y1, y0, z, c)
            ).start()
        pltpu.make_async_copy(st_sub(x, j), sub(l1, x, j), l1r.at[j, 3]).start()

    def leg1_wait(j):
        for i, xx in enumerate(xs):
            remote(st_sub(xx, j), sub(l1, xx, j), l1s.at[j], l1r.at[j, i], sib).wait_recv()
        pltpu.make_async_copy(st_sub(x, j), sub(l1, x, j), l1r.at[j, 3]).wait()

    relay = y0 == z1

    def leg2_start(j):
        there = y1 * 2 + z2
        if j % 2:
            for s in range(4):
                dest, own = leg2(s)

                @pl.when(jnp.logical_not(own))
                def _(dest=dest, s=s):
                    remote(
                        sub(l1, s, j), sub(l2, there, j), l2s.at[j], l2r.at[j, there], dest
                    ).start()

                @pl.when(own)
                def _(s=s):
                    pltpu.make_async_copy(sub(l1, s, j), sub(l2, s, j), l2r.at[j, s]).start()

            return
        for s in range(4):
            s1, s0 = s // 2, s % 2
            stays = relay & (y1 == s1)
            slot = (y1 * 2 + y0) * 2 + s0

            @pl.when(jnp.logical_not(stays))
            def _(s=s, s1=s1, slot=slot):
                remote(
                    sub(l1, s, j), rel.at[j // 2, slot], l2as.at[j // 2], l2ar.at[j // 2, slot],
                    device(x, s1, z1, z, c),
                ).start()

            @pl.when(stays)
            def _(s=s, slot=slot):
                pltpu.make_async_copy(
                    sub(l1, s, j), rel.at[j // 2, slot], l2ar.at[j // 2, slot]
                ).start()

    def leg2_relay(j):
        @pl.when(relay)
        def _():
            for ysrc in range(4):
                for s0 in range(2):
                    slot = ysrc * 2 + s0
                    here = rel.at[j // 2, slot]
                    t = (ysrc // 2) * 2 + z2
                    remote(here, here, l2as.at[j // 2], l2ar.at[j // 2, slot], sib).wait_recv()
                    stays = (z2 == s0) & (z1 == ysrc % 2)

                    @pl.when(jnp.logical_not(stays))
                    def _(here=here, t=t, s0=s0, ysrc=ysrc):
                        remote(
                            here, sub(l2, t, j), l2s.at[j], l2r.at[j, t],
                            device(x, y1, y0, s0 * 4 + (ysrc % 2) * 2 + z0, c),
                        ).start()

                    @pl.when(stays)
                    def _(here=here, t=t):
                        pltpu.make_async_copy(here, sub(l2, t, j), l2r.at[j, t]).start()

    def leg2_wait(j):
        for s in range(4):
            remote(sub(l1, s, j), sub(l2, s, j), l2s.at[j], l2r.at[j, s], sib).wait_recv()

    def fin_sub(chunk, j):
        return fin.at[pl.ds(chunk * BLK + j * rows_sub, rows_sub)]

    def leg3_start(j):
        for i, xx in enumerate(xs):
            remote(
                sub(l2, xx, j), fin_sub(x, j), l3s.at[j], l3r.at[j, 3 - 1 - i], device(xx, y1, y0, z, c)
            ).start()
        pltpu.make_async_copy(sub(l2, x, j), fin_sub(x, j), l3r.at[j, 3]).start()

    def leg3_wait(j):
        for i, xx in enumerate(xs):
            remote(sub(l2, xx, j), fin_sub(xx, j), l3s.at[j], l3r.at[j, i], sib).wait_recv()
        pltpu.make_async_copy(sub(l2, x, j), fin_sub(x, j), l3r.at[j, 3]).wait()

    def legs_drain():
        rows = pl.ds(0, rows_sub)

        def gone(n, sem):
            ref = l1.at[pl.ds(0, n), rows] if n <= 4 else rel.at[0, pl.ds(0, n)]
            remote(ref, ref, sem, l1r.at[0, 0], sib).wait_send()

        for j in range(SUB):
            gone(3, l1s.at[j])
            gone(3, l3s.at[j])

            @pl.when(relay)
            def _(j=j):
                if j % 2:
                    gone(3, l2s.at[j])
                else:
                    gone(2, l2as.at[j // 2])
                    gone(6, l2s.at[j])

            @pl.when(jnp.logical_not(relay))
            def _(j=j):
                if j % 2:
                    gone(4, l2s.at[j])
                else:
                    gone(4, l2as.at[j // 2])

    def swap_start(i, src, dst):
        @pl.when(not_diag)
        def _():
            remote(src, dst, ms.at[i], mr.at[i], mirror).start()

        @pl.when(diag)
        def _():
            pltpu.make_async_copy(src, dst, mr.at[i]).start()

    def swap_wait(i, src, dst):
        @pl.when(not_diag)
        def _():
            remote(src, dst, ms.at[i], mr.at[i], mirror).wait_recv()

        @pl.when(diag)
        def _():
            pltpu.make_async_copy(src, dst, mr.at[i]).wait()

    def swap_drain(i, src, dst):
        @pl.when(not_diag)
        def _():
            remote(src, dst, ms.at[i], mr.at[i], mirror).wait_send()

    def triplets(g, out):
        live = cnt_s[0]
        zero = jnp.zeros((T, BLK), BF16)
        for b in range(NB):
            blk = g[src_s[b]]
            tb = jnp.where(b < live, tgt_s[b], -1)
            for o in range(4):
                lhs[o * T : (o + 1) * T, b * BLK : (b + 1) * BLK] = jnp.where(tb == o, blk, zero)
        acc = jnp.dot(lhs[...], coef[...].reshape(NB * BLK, BLK), preferred_element_type=F32)
        for o in range(4):
            out[:, o * BLK : (o + 1) * BLK] = acc[o * T : (o + 1) * T].astype(BF16)

    def permute_t(val):
        return jnp.dot(val, perm[...], preferred_element_type=F32)

    def layer(l, rows_ref, agg, sum_ref, br):
        def body(r, _):
            for i in range(2):
                rows = pl.ds(pl.multiple_of(r * 256 + i * BLK, BLK), BLK)
                up = lax.dot_general(
                    agg[:, rows], wup[l], (((0,), (0,)), ((), ())), preferred_element_type=F32
                )
                s = rows_ref[rows, :].astype(F32) + up
                sum_ref[rows, :] = s
                scale = lax.rsqrt(jnp.mean(s * s, axis=-1, keepdims=True) + 1e-06)
                nrm[rows, :] = (gain_ref[l : l + 1, :] * s * scale).astype(BF16)
            rows = pl.ds(pl.multiple_of(r * 256, 256), 256)
            h = jnp.dot(nrm[rows, :], win[l], preferred_element_type=F32)
            h = 0.5 * h
            act[rows, :] = (h + h * jnp.tanh(h)).astype(BF16)
            br[rows, :] = jnp.dot(
                act[rows, :], wout[l], preferred_element_type=F32
            ).astype(BF16)
            return 0

        lax.fori_loop(0, 2, body, 0)

    def by_rows(f):
        def body(r, _):
            f(pl.ds(pl.multiple_of(r * BLK, BLK), BLK))
            return 0

        lax.fori_loop(0, 4, body, 0)

    for j in range(SUB):
        leg1_start(j)

    def onehot(rows, r):
        ids = lax.broadcasted_iota(jnp.int32, (BLK, E), 0) + r * BLK
        perm[rows, :] = jnp.where(ids == rs_ref[0:1, :], 1.0, 0.0).astype(BF16)

    def onehot_body(r, _):
        onehot(pl.ds(pl.multiple_of(r * BLK, BLK), BLK), r)
        return 0

    lax.fori_loop(0, 4, onehot_body, 0)

    start, z_step, y_step, finish, drain0 = gat0
    z_step(1, 0)
    z_step(1, 1)
    y_step(0, 0)
    y_step(0, 1)
    z_step(2, 0)
    z_step(2, 1)
    y_step(1, 0)
    y_step(1, 1)
    leg1_wait(0)
    leg2_start(0)
    z_step(3, 0)
    z_step(3, 1)
    y_step(2, 0)
    y_step(2, 1)
    leg1_wait(1)
    leg2_start(1)
    z_step(4, 0)
    z_step(4, 1)
    y_step(3, 0)
    y_step(3, 1)
    leg1_wait(2)
    leg2_start(2)
    leg2_relay(0)
    y_step(4, 0)
    y_step(4, 1)
    finish()

    loads[2].wait()
    triplets(g0, aggt.at[0])
    swap_start(0, aggt.at[0], aggm.at[0])
    leg1_wait(3)
    leg2_start(3)
    leg2_relay(2)
    for i in (3, 4, 5):
        loads[i].wait()
    layer(0, st, aggt.at[0], summed, branch)
    pbt[...] = proj_t(1, branch[...]).astype(BF16)
    swap_start(1, pbt, pbm)

    def part_sum(rows):
        nrm[rows, :] = (summed[rows, :] + branch[rows, :].astype(F32)).astype(BF16)

    by_rows(part_sum)
    half1 = proj_t(1, nrm[...])
    leg2_wait(0)
    leg3_start(0)
    leg2_wait(1)
    leg3_start(1)
    swap_wait(1, pbt, pbm)
    put_own(g1, half1 + permute_t(pbm[...]))
    start, z_step, y_step, finish, drain1 = gat1
    start()
    z_step(1, 0)
    z_step(1, 1)
    y_step(0, 0)
    y_step(0, 1)
    leg2_wait(2)
    leg3_start(2)
    z_step(2, 0)
    z_step(2, 1)
    y_step(1, 0)
    y_step(1, 1)
    leg2_wait(3)
    leg3_start(3)
    z_step(3, 0)
    z_step(3, 1)
    y_step(2, 0)
    y_step(2, 1)
    z_step(4, 0)
    z_step(4, 1)
    y_step(3, 0)
    y_step(3, 1)
    y_step(4, 0)
    y_step(4, 1)

    swap_wait(0, aggt.at[0], aggm.at[0])
    act[0:T, 0:E] = permute_t(aggm[0]).astype(BF16)
    aggm[0] = act[0:T, 0:E]
    for j in range(SUB):
        leg3_wait(j)

    def take_rows(r, _):
        rows = pl.ds(pl.multiple_of(r * 256, 256), 256)
        mst[rows, :] = lax.dot_general(
            perm[:, rows], fin[...], (((0,), (0,)), ((), ())), preferred_element_type=F32
        ).astype(BF16)
        return 0

    lax.fori_loop(0, 2, take_rows, 0)
    finish()
    triplets(g1, aggt.at[1])
    swap_start(2, aggt.at[1], aggm.at[1])
    layer(0, mst, aggm.at[0], msum, mbr)

    def next_state(rows):
        b = branch[rows, :].astype(F32)
        m = mbr[rows, :].astype(F32)
        st[rows, :] = ((summed[rows, :] + b) + m).astype(BF16)
        mst[rows, :] = ((msum[rows, :] + m) + b).astype(BF16)

    legs_drain()
    by_rows(next_state)

    for i in (6, 7):
        loads[i].wait()
    layer(1, st, aggt.at[1], summed, branch)
    swap_wait(2, aggt.at[1], aggm.at[1])
    act[0:T, 0:E] = permute_t(aggm[1]).astype(BF16)
    aggm[1] = act[0:T, 0:E]
    layer(1, mst, aggm.at[1], msum, mbr)

    def final(rows):
        out_ref[rows, :] = (
            (summed[rows, :] + branch[rows, :].astype(F32)) + mbr[rows, :].astype(F32)
        ).astype(BF16)

    by_rows(final)

    drain0()
    drain1()
    swap_drain(0, aggt.at[0], aggm.at[0])
    swap_drain(1, pbt, pbm)
    swap_drain(2, aggt.at[1], aggm.at[1])


def local(
    edge_states, triplet_coeff, block_target, block_source, block_count, reverse_slot,
    w_proj, w_up, w_in, w_out, norm_gain,
):
    vmem = pl.BlockSpec(memory_space=pltpu.VMEM)
    smem = pl.BlockSpec(memory_space=pltpu.SMEM)
    hbm = pl.BlockSpec(memory_space=pltpu.HBM)
    dma = pltpu.SemaphoreType.DMA
    out = pl.pallas_call(
        kernel,
        out_shape=jax.ShapeDtypeStruct((E, D), BF16),
        in_specs=[smem, smem, smem, hbm, hbm, vmem, hbm, hbm, hbm, hbm, vmem],
        out_specs=vmem,
        scratch_shapes=[
            pltpu.VMEM((E, D), BF16),
            pltpu.VMEM((NB, BLK, BLK), BF16),
            pltpu.VMEM((2, T, D), BF16),
            pltpu.VMEM((2, T, D), BF16),
            pltpu.VMEM((2, D, D), BF16),
            pltpu.VMEM((2, D, D), BF16),
            pltpu.VMEM((NBLK, T, BLK), BF16),
            pltpu.VMEM((NBLK, T, BLK), BF16),
            pltpu.VMEM((4, BLK, D), BF16),
            pltpu.VMEM((4, BLK, D), BF16),
            pltpu.VMEM((SUB // 2, 8, ROWS, D), BF16),
            pltpu.VMEM((E, D), BF16),
            pltpu.VMEM((E, E), BF16),
            pltpu.VMEM((4 * T, NB * BLK), BF16),
            pltpu.VMEM((2, T, E), BF16),
            pltpu.VMEM((2, T, E), BF16),
            pltpu.VMEM((T, E), BF16),
            pltpu.VMEM((T, E), BF16),
            pltpu.VMEM((E, D), F32),
            pltpu.VMEM((E, D), BF16),
            pltpu.VMEM((E, D), BF16),
            pltpu.VMEM((E, D), F32),
            pltpu.VMEM((E, D), BF16),
            pltpu.VMEM((E, D), BF16),
            pltpu.VMEM((E, D), BF16),
            dma((8,)),
            dma((2,)),
            dma((2, 9, 2)),
            dma((2, 2, 4, 2)),
            dma((2,)),
            dma((SUB,)), dma((SUB, 4)),
            dma((SUB,)), dma((SUB, 4)),
            dma((SUB // 2,)), dma((SUB // 2, 8)),
            dma((SUB,)), dma((SUB, 4)),
            dma((3,)), dma((3,)),
        ],
        compiler_params=pltpu.CompilerParams(
            collective_id=0, has_side_effects=True, vmem_limit_bytes=50 << 20
        ),
        name="edge_layers",
    )(
        block_target[0, 0], block_source[0, 0], block_count[0], edge_states[0, 0],
        triplet_coeff[0, 0], reverse_slot[0], jnp.swapaxes(w_proj, 1, 2), w_up, w_in, w_out,
        norm_gain,
    )
    return out[None, None]


def solution(mesh):
    return jax.shard_map(
        local,
        mesh=mesh,
        in_specs=(
            P("src", "tgt", None, None),
            P("src", "tgt", None, None, None),
            P("src", "tgt", None),
            P("src", "tgt", None),
            P("src", "tgt"),
            P("src", "tgt", None),
            P(),
            P(),
            P(),
            P(),
            P(),
        ),
        out_specs=P("src", "tgt", None, None),
        check_vma=False,
    )
```

```python
import functools

import jax
import jax.numpy as jnp
from jax import lax
from jax.experimental import pallas as pl
from jax.experimental.pallas import tpu as pltpu
from jax.sharding import PartitionSpec as P

MESH = pl.DeviceIdType.MESH
BF16 = jnp.bfloat16
F32 = jnp.float32
D = 1024
E = 512
T = 64
BLK = 128
NB = 16
SUB = 4
ROWS = BLK // SUB
NBLK = 128


def place():
    s = lax.axis_index("src")
    t = lax.axis_index("tgt")
    return dict(y1=s // 16, z=(s // 2) % 8, c=s % 2, x=t // 2, y0=t % 2)


def device(x, y1, y0, z, c):
    return (y1 * 16 + z * 2 + c, x * 2 + y0)


def kernel(
    tgt_s, src_s, cnt_s, st_h, coef_h, rs_ref, wp_h, wup_h, win_h, wout_h, gain_ref, out_ref,
    st, coef, wp, wup, win, wout, g0, g1, l1, l2, rel, fin, perm, lhs, aggt, aggm, pbt, pbm,
    summed, branch, mst, msum, mbr, nrm, act, lsem,
    gs, yr, zr, sr, l1s, l1r, l2s, l2r, l2as, l2ar, l3s, l3r, ms, mr,
):
    k = place()
    x, y1, y0, z, c = k["x"], k["y1"], k["y0"], k["z"], k["c"]
    z2, z1, z0 = z // 4, (z // 2) % 2, z % 2
    x1, x0 = x // 2, x % 2
    me_slot = y1 * 16 + z * 2 + c

    sib = device(x, y1, y0, z, 1 - c)
    ypart = device(x, 1 - y1, y0, z, c)
    zup = device(x, y1, y0, (z + 1) % 8, c)
    zdn = device(x, y1, y0, (z + 7) % 8, c)
    mirror = device(y1 * 2 + z2, x1, z1, x0 * 4 + y0 * 2 + z0, c)
    diag = (x1 == y1) & (x0 == z2) & (y0 == z1)
    not_diag = jnp.logical_not(diag)

    def leg2(s):
        s1, s0 = s // 2, s % 2
        dest = device(x, s1, z1, s0 * 4 + y0 * 2 + z0, c)
        own = (y1 == s1) & (y0 == z1) & (z2 == s0)
        return dest, own

    xs = [(x + i) % 4 for i in range(1, 4)]

    bar = pltpu.get_barrier_semaphore()

    def signal(d):
        pl.semaphore_signal(bar, inc=1, device_id=d, device_id_type=MESH)

    @pl.when(not_diag)
    def _():
        signal(mirror)

    for s in range(4):
        dest, own = leg2(s)

        @pl.when(jnp.logical_not(own))
        def _(dest=dest):
            signal(dest)

    ys = [(y1 * 2 + y0 + i) % 4 for i in range(1, 4)]
    for yy in ys:
        signal(device(x, yy // 2, yy % 2, z, c))
    for i in (1, 2, 4, 6, 7):
        signal(device(x, y1, y0, (z + i) % 8, c))
    signal(sib)
    for xx in xs:
        signal(device(xx, y1, y0, z, c))

    loads = [
        pltpu.make_async_copy(a, b, lsem.at[i])
        for i, (a, b) in enumerate(
            [(st_h, st), (wp_h, wp), (coef_h, coef), (wup_h, wup), (win_h.at[0], win.at[0]),
             (wout_h.at[0], wout.at[0]), (win_h.at[1], win.at[1]), (wout_h.at[1], wout.at[1])]
        )
    ]
    for cp in loads:
        cp.start()

    loads[0].wait()
    loads[1].wait()

    def proj_t(l, rows):
        return lax.dot_general(
            wp[l], rows, (((1,), (1,)), ((), ())), preferred_element_type=F32
        )

    def put_own(g, val):
        for b in range(4):
            g[me_slot * 4 + b] = val[:, b * BLK : (b + 1) * BLK].astype(BF16)

    put_own(g0, proj_t(0, st[...]))

    n_own2 = (y0 == z1).astype(jnp.int32)
    pl.semaphore_wait(bar, 9 + 3 + 4 - n_own2 + not_diag.astype(jnp.int32))

    def remote(src, dst, ss, rs, d):
        return pltpu.make_async_remote_copy(
            src_ref=src, dst_ref=dst, send_sem=ss, recv_sem=rs, device_id=d, device_id_type=MESH
        )

    zup2 = device(x, y1, y0, (z + 2) % 8, c)
    zdn2 = device(x, y1, y0, (z + 6) % 8, c)

    def make_gather(l, g):
        def half(kind, zz):
            col = 1 - y1 if kind == 2 else y1
            return g.at[pl.ds((col * 16 + zz * 2 + c) * 4 + 2 * (kind % 2), 2)]

        def other(zz):
            return g.at[pl.ds(((1 - y1) * 16 + zz * 2 + c) * 4 + 2, 2)]

        def origin(direction, dist):
            return (z + 8 - dist) % 8 if direction == 0 else (z + dist) % 8

        def to_sib(p):
            remote(p, p, gs.at[l], sr.at[l], sib).start()

        def z_copy(p, direction, dist, kind):
            if dist == 4:
                d = zup2 if direction == 0 else zdn2
            else:
                d = zup if direction == 0 else zdn
            return remote(p, p, gs.at[l], zr.at[l, direction, dist - 1, kind], d)

        def y_copy(p, direction, dist, h):
            i = dist if direction == 0 or dist == 0 else 4 + dist
            return remote(p, p, gs.at[l], yr.at[l, i, h], ypart)

        def ways(dist, kind):
            return (0, 1) if dist < 4 else ((0,) if kind == 0 else (1,))

        def start():
            for kind in (0, 1):
                own = half(kind, z)
                for direction in (0, 1):
                    z_copy(own, direction, 1, kind).start()
                y_copy(own, 0, 0, kind).start()
                to_sib(own)

        def z_step(dist, kinds=(0, 1, 2)):
            for kind in kinds:
                for direction in ways(dist, kind):
                    got = half(kind, origin(direction, dist))
                    z_copy(got, direction, dist, kind).wait_recv()
                    if dist < 3:
                        z_copy(got, direction, dist + 1, kind).start()
                    if dist == 2 and direction in ways(4, kind):
                        z_copy(got, direction, 4, kind).start()
                    if kind == 1:
                        y_copy(got, direction, dist, 1).start()
                    to_sib(got)

        def y_first():
            got = half(2, z)
            y_copy(got, 0, 0, 0).wait_recv()
            for direction in (0, 1):
                z_copy(got, direction, 1, 2).start()
            to_sib(got)

        def y_step(dist):
            for direction in ways(dist, 1) if dist else (0,):
                got = other(origin(direction, dist))
                y_copy(got, direction, dist, 1).wait_recv()
                to_sib(got)

        def finish():
            all_sib = g.at[pl.ds(0, 64)]
            remote(all_sib, all_sib, gs.at[l], sr.at[l], sib).wait_recv()

        def drain():
            a = g.at[pl.ds(0, 4 * 31)]
            remote(a, a, gs.at[l], sr.at[l], sib).wait_send()

        return start, z_step, y_first, y_step, finish, drain

    gat0 = make_gather(0, g0)
    gat1 = make_gather(1, g1)
    gat0[0]()

    rows_sub = ROWS

    def sub(ref, slot, j):
        return ref.at[slot, pl.ds(j * rows_sub, rows_sub)]

    def st_sub(chunk, j):
        return st.at[pl.ds(chunk * BLK + j * rows_sub, rows_sub)]

    def leg1_start(j):
        for i, xx in enumerate(xs):
            remote(
                st_sub(xx, j), sub(l1, x, j), l1s.at[j], l1r.at[j, 3 - 1 - i], device(xx, y1, y0, z, c)
            ).start()

    def leg1_wait(j):
        for i, xx in enumerate(xs):
            remote(st_sub(xx, j), sub(l1, xx, j), l1s.at[j], l1r.at[j, i], sib).wait_recv()

    relay = y0 == z1

    def leg2_one(j, s, src):
        there = y1 * 2 + z2
        s1, s0 = s // 2, s % 2
        if j % 2:
            dest, own = leg2(s)

            @pl.when(jnp.logical_not(own))
            def _():
                remote(src, sub(l2, there, j), l2s.at[j], l2r.at[j, there], dest).start()

            @pl.when(own)
            def _():
                pltpu.make_async_copy(src, sub(l2, s, j), l2r.at[j, s]).start()

            return
        stays = relay & (y1 == s1)
        slot = (y1 * 2 + y0) * 2 + s0

        @pl.when(jnp.logical_not(stays))
        def _():
            remote(
                src, rel.at[j // 2, slot], l2as.at[j // 2], l2ar.at[j // 2, slot],
                device(x, s1, z1, z, c),
            ).start()

        @pl.when(stays)
        def _():
            pltpu.make_async_copy(src, rel.at[j // 2, slot], l2ar.at[j // 2, slot]).start()

    def leg2_own(j):
        leg2_one(j, x, st_sub(x, j))

    def leg2_start(j):
        for xx in xs:
            leg2_one(j, xx, sub(l1, xx, j))

    def leg2_relay(j):
        @pl.when(relay)
        def _():
            for ysrc in range(4):
                for s0 in range(2):
                    slot = ysrc * 2 + s0
                    here = rel.at[j // 2, slot]
                    t = (ysrc // 2) * 2 + z2
                    remote(here, here, l2as.at[j // 2], l2ar.at[j // 2, slot], sib).wait_recv()
                    stays = (z2 == s0) & (z1 == ysrc % 2)

                    @pl.when(jnp.logical_not(stays))
                    def _(here=here, t=t, s0=s0, ysrc=ysrc):
                        remote(
                            here, sub(l2, t, j), l2s.at[j], l2r.at[j, t],
                            device(x, y1, y0, s0 * 4 + (ysrc % 2) * 2 + z0, c),
                        ).start()

                    @pl.when(stays)
                    def _(here=here, t=t):
                        pltpu.make_async_copy(here, sub(l2, t, j), l2r.at[j, t]).start()

    def leg2_wait(j):
        for s in range(4):
            remote(sub(l1, s, j), sub(l2, s, j), l2s.at[j], l2r.at[j, s], sib).wait_recv()

    def fin_sub(chunk, j):
        return fin.at[pl.ds(chunk * BLK + j * rows_sub, rows_sub)]

    def leg3_start(j):
        for i, xx in enumerate(xs):
            remote(
                sub(l2, xx, j), fin_sub(x, j), l3s.at[j], l3r.at[j, 3 - 1 - i], device(xx, y1, y0, z, c)
            ).start()
        pltpu.make_async_copy(sub(l2, x, j), fin_sub(x, j), l3r.at[j, 3]).start()

    def leg3_wait(j):
        for i, xx in enumerate(xs):
            remote(sub(l2, xx, j), fin_sub(xx, j), l3s.at[j], l3r.at[j, i], sib).wait_recv()
        pltpu.make_async_copy(sub(l2, x, j), fin_sub(x, j), l3r.at[j, 3]).wait()

    def legs_drain():
        rows = pl.ds(0, rows_sub)

        def gone(n, sem):
            ref = l1.at[pl.ds(0, n), rows] if n <= 4 else rel.at[0, pl.ds(0, n)]
            remote(ref, ref, sem, l1r.at[0, 0], sib).wait_send()

        for j in range(SUB):
            gone(3, l1s.at[j])
            gone(3, l3s.at[j])

            @pl.when(relay)
            def _(j=j):
                if j % 2:
                    gone(3, l2s.at[j])
                else:
                    gone(2, l2as.at[j // 2])
                    gone(6, l2s.at[j])

            @pl.when(jnp.logical_not(relay))
            def _(j=j):
                if j % 2:
                    gone(4, l2s.at[j])
                else:
                    gone(4, l2as.at[j // 2])

    def swap_start(i, src, dst):
        @pl.when(not_diag)
        def _():
            remote(src, dst, ms.at[i], mr.at[i], mirror).start()

        @pl.when(diag)
        def _():
            pltpu.make_async_copy(src, dst, mr.at[i]).start()

    def swap_wait(i, src, dst):
        @pl.when(not_diag)
        def _():
            remote(src, dst, ms.at[i], mr.at[i], mirror).wait_recv()

        @pl.when(diag)
        def _():
            pltpu.make_async_copy(src, dst, mr.at[i]).wait()

    def swap_drain(i, src, dst):
        @pl.when(not_diag)
        def _():
            remote(src, dst, ms.at[i], mr.at[i], mirror).wait_send()

    def triplets(g, out):
        live = cnt_s[0]
        zero = jnp.zeros((T, BLK), BF16)
        for b in range(NB):
            blk = g[src_s[b]]
            tb = jnp.where(b < live, tgt_s[b], -1)
            for o in range(4):
                lhs[o * T : (o + 1) * T, b * BLK : (b + 1) * BLK] = jnp.where(tb == o, blk, zero)
        acc = jnp.dot(lhs[...], coef[...].reshape(NB * BLK, BLK), preferred_element_type=F32)
        for o in range(4):
            out[:, o * BLK : (o + 1) * BLK] = acc[o * T : (o + 1) * T].astype(BF16)

    def permute_t(val):
        return jnp.dot(val, perm[...], preferred_element_type=F32)

    def layer_half(l, rows_ref, agg, sum_ref, br, r):
        def norm(i, _):
            rows = pl.ds(pl.multiple_of(r * 256 + i * BLK, BLK), BLK)
            up = lax.dot_general(
                agg[:, rows], wup[l], (((0,), (0,)), ((), ())), preferred_element_type=F32
            )
            s = rows_ref[rows, :].astype(F32) + up
            sum_ref[rows, :] = s
            scale = lax.rsqrt(jnp.mean(s * s, axis=-1, keepdims=True) + 1e-06)
            nrm[rows, :] = (gain_ref[l : l + 1, :] * s * scale).astype(BF16)
            return 0

        for i in range(2):
            norm(i, 0)
        rows = pl.ds(r * 256 if isinstance(r, int) else pl.multiple_of(r * 256, 256), 256)
        h = jnp.dot(nrm[rows, :], win[l], preferred_element_type=F32)
        h = 0.5 * h
        act[rows, :] = (h + h * jnp.tanh(h)).astype(BF16)
        br[rows, :] = jnp.dot(act[rows, :], wout[l], preferred_element_type=F32).astype(BF16)

    def layer(l, rows_ref, agg, sum_ref, br):
        def body(r, _):
            layer_half(l, rows_ref, agg, sum_ref, br, r)
            return 0

        lax.fori_loop(0, 2, body, 0)

    def by_rows(f):
        def body(r, _):
            f(pl.ds(pl.multiple_of(r * BLK, BLK), BLK))
            return 0

        lax.fori_loop(0, 4, body, 0)

    for j in range(SUB):
        leg1_start(j)

    def onehot(rows, r):
        ids = lax.broadcasted_iota(jnp.int32, (BLK, E), 0) + r * BLK
        perm[rows, :] = jnp.where(ids == rs_ref[0:1, :], 1.0, 0.0).astype(BF16)

    def onehot_body(r, _):
        onehot(pl.ds(pl.multiple_of(r * BLK, BLK), BLK), r)
        return 0

    lax.fori_loop(0, 4, onehot_body, 0)

    _, z_step, y_first, y_step, finish, drain0 = gat0
    z_step(1, (0, 1))
    leg2_own(0)
    leg2_own(1)
    y_first()
    y_step(0)
    z_step(2, (0, 1))
    z_step(1, (2,))
    leg1_wait(0)
    leg2_start(0)
    z_step(2, (2,))
    y_step(1)
    leg2_own(2)
    leg2_own(3)
    leg1_wait(1)
    leg2_start(1)
    z_step(3)
    y_step(2)
    leg1_wait(2)
    leg2_start(2)
    leg2_relay(0)
    z_step(4)
    y_step(3)
    leg1_wait(3)
    leg2_start(3)
    y_step(4)
    finish()

    loads[2].wait()
    triplets(g0, aggt.at[0])
    swap_start(0, aggt.at[0], aggm.at[0])
    leg2_relay(2)
    for i in (3, 4, 5):
        loads[i].wait()
    layer_half(0, st, aggt.at[0], summed, branch, 0)
    leg2_wait(0)
    leg3_start(0)
    layer_half(0, st, aggt.at[0], summed, branch, 1)
    pbt[...] = proj_t(1, branch[...]).astype(BF16)
    swap_start(1, pbt, pbm)
    leg2_wait(1)
    leg3_start(1)

    def part_sum(rows):
        nrm[rows, :] = (summed[rows, :] + branch[rows, :].astype(F32)).astype(BF16)

    by_rows(part_sum)
    half1 = proj_t(1, nrm[...])
    leg2_wait(2)
    leg3_start(2)
    swap_wait(1, pbt, pbm)
    put_own(g1, half1 + permute_t(pbm[...]))
    start, z_step, y_first, y_step, finish, drain1 = gat1
    start()
    z_step(1, (0, 1))
    y_first()
    y_step(0)
    z_step(2, (0, 1))
    z_step(1, (2,))
    leg2_wait(3)
    leg3_start(3)
    z_step(2, (2,))
    y_step(1)
    z_step(3)
    y_step(2)
    z_step(4)
    y_step(3)
    y_step(4)

    swap_wait(0, aggt.at[0], aggm.at[0])
    act[0:T, 0:E] = permute_t(aggm[0]).astype(BF16)
    aggm[0] = act[0:T, 0:E]
    for j in range(SUB):
        leg3_wait(j)

    def take_rows(r, _):
        rows = pl.ds(pl.multiple_of(r * 256, 256), 256)
        mst[rows, :] = lax.dot_general(
            perm[:, rows], fin[...], (((0,), (0,)), ((), ())), preferred_element_type=F32
        ).astype(BF16)
        return 0

    lax.fori_loop(0, 2, take_rows, 0)
    finish()
    triplets(g1, aggt.at[1])
    swap_start(2, aggt.at[1], aggm.at[1])
    layer(0, mst, aggm.at[0], msum, mbr)

    def next_state(rows):
        b = branch[rows, :].astype(F32)
        m = mbr[rows, :].astype(F32)
        st[rows, :] = ((summed[rows, :] + b) + m).astype(BF16)
        mst[rows, :] = ((msum[rows, :] + m) + b).astype(BF16)

    legs_drain()
    by_rows(next_state)

    for i in (6, 7):
        loads[i].wait()
    layer(1, st, aggt.at[1], summed, branch)
    swap_wait(2, aggt.at[1], aggm.at[1])
    act[0:T, 0:E] = permute_t(aggm[1]).astype(BF16)
    aggm[1] = act[0:T, 0:E]
    layer(1, mst, aggm.at[1], msum, mbr)

    def final(rows):
        out_ref[rows, :] = (
            (summed[rows, :] + branch[rows, :].astype(F32)) + mbr[rows, :].astype(F32)
        ).astype(BF16)

    by_rows(final)

    drain0()
    drain1()
    swap_drain(0, aggt.at[0], aggm.at[0])
    swap_drain(1, pbt, pbm)
    swap_drain(2, aggt.at[1], aggm.at[1])


def local(
    edge_states, triplet_coeff, block_target, block_source, block_count, reverse_slot,
    w_proj, w_up, w_in, w_out, norm_gain,
):
    vmem = pl.BlockSpec(memory_space=pltpu.VMEM)
    smem = pl.BlockSpec(memory_space=pltpu.SMEM)
    hbm = pl.BlockSpec(memory_space=pltpu.HBM)
    dma = pltpu.SemaphoreType.DMA
    out = pl.pallas_call(
        kernel,
        out_shape=jax.ShapeDtypeStruct((E, D), BF16),
        in_specs=[smem, smem, smem, hbm, hbm, vmem, hbm, hbm, hbm, hbm, vmem],
        out_specs=vmem,
        scratch_shapes=[
            pltpu.VMEM((E, D), BF16),
            pltpu.VMEM((NB, BLK, BLK), BF16),
            pltpu.VMEM((2, T, D), BF16),
            pltpu.VMEM((2, T, D), BF16),
            pltpu.VMEM((2, D, D), BF16),
            pltpu.VMEM((2, D, D), BF16),
            pltpu.VMEM((NBLK, T, BLK), BF16),
            pltpu.VMEM((NBLK, T, BLK), BF16),
            pltpu.VMEM((4, BLK, D), BF16),
            pltpu.VMEM((4, BLK, D), BF16),
            pltpu.VMEM((SUB // 2, 8, ROWS, D), BF16),
            pltpu.VMEM((E, D), BF16),
            pltpu.VMEM((E, E), BF16),
            pltpu.VMEM((4 * T, NB * BLK), BF16),
            pltpu.VMEM((2, T, E), BF16),
            pltpu.VMEM((2, T, E), BF16),
            pltpu.VMEM((T, E), BF16),
            pltpu.VMEM((T, E), BF16),
            pltpu.VMEM((E, D), F32),
            pltpu.VMEM((E, D), BF16),
            pltpu.VMEM((E, D), BF16),
            pltpu.VMEM((E, D), F32),
            pltpu.VMEM((E, D), BF16),
            pltpu.VMEM((E, D), BF16),
            pltpu.VMEM((E, D), BF16),
            dma((8,)),
            dma((2,)),
            dma((2, 9, 2)),
            dma((2, 2, 4, 3)),
            dma((2,)),
            dma((SUB,)), dma((SUB, 4)),
            dma((SUB,)), dma((SUB, 4)),
            dma((SUB // 2,)), dma((SUB // 2, 8)),
            dma((SUB,)), dma((SUB, 4)),
            dma((3,)), dma((3,)),
        ],
        compiler_params=pltpu.CompilerParams(
            collective_id=0, has_side_effects=True, vmem_limit_bytes=56 << 20
        ),
        name="edge_layers",
    )(
        block_target[0, 0], block_source[0, 0], block_count[0], edge_states[0, 0],
        triplet_coeff[0, 0], reverse_slot[0], jnp.swapaxes(w_proj, 1, 2), w_up, w_in, w_out,
        norm_gain,
    )
    return out[None, None]


def solution(mesh):
    return jax.shard_map(
        local,
        mesh=mesh,
        in_specs=(
            P("src", "tgt", None, None),
            P("src", "tgt", None, None, None),
            P("src", "tgt", None),
            P("src", "tgt", None),
            P("src", "tgt"),
            P("src", "tgt", None),
            P(),
            P(),
            P(),
            P(),
            P(),
        ),
        out_specs=P("src", "tgt", None, None),
        check_vma=False,
    )
```

```python
import functools

import jax
import jax.numpy as jnp
from jax import lax
from jax.experimental import pallas as pl
from jax.experimental.pallas import tpu as pltpu
from jax.sharding import PartitionSpec as P

MESH = pl.DeviceIdType.MESH
BF16 = jnp.bfloat16
F32 = jnp.float32
D = 1024
E = 512
T = 64
BLK = 128
NB = 16
SUB = 4
ROWS = BLK // SUB
NBLK = 128


def place():
    s = lax.axis_index("src")
    t = lax.axis_index("tgt")
    return dict(y1=s // 16, z=(s // 2) % 8, c=s % 2, x=t // 2, y0=t % 2)


def device(x, y1, y0, z, c):
    return (y1 * 16 + z * 2 + c, x * 2 + y0)


def kernel(
    tgt_s, src_s, cnt_s, st_h, coef_h, rs_ref, wp_h, wup_h, win_h, wout_h, gain_ref, out_ref,
    st, coef, wp, wup, win, wout, g0, g1, l1, l2, rel, fin, perm, lhs, aggt, aggm, pbt, pbm,
    summed, branch, mst, msum, mbr, nrm, act, lsem,
    gs, yr, zr, sr, l1s, l1r, l2s, l2r, l2as, l2ar, l3s, l3r, ms, mr,
):
    k = place()
    x, y1, y0, z, c = k["x"], k["y1"], k["y0"], k["z"], k["c"]
    z2, z1, z0 = z // 4, (z // 2) % 2, z % 2
    x1, x0 = x // 2, x % 2
    me_slot = y1 * 16 + z * 2 + c

    sib = device(x, y1, y0, z, 1 - c)
    ypart = device(x, 1 - y1, y0, z, c)
    zup = device(x, y1, y0, (z + 1) % 8, c)
    zdn = device(x, y1, y0, (z + 7) % 8, c)
    mirror = device(y1 * 2 + z2, x1, z1, x0 * 4 + y0 * 2 + z0, c)
    diag = (x1 == y1) & (x0 == z2) & (y0 == z1)
    not_diag = jnp.logical_not(diag)

    def leg2(s):
        s1, s0 = s // 2, s % 2
        dest = device(x, s1, z1, s0 * 4 + y0 * 2 + z0, c)
        own = (y1 == s1) & (y0 == z1) & (z2 == s0)
        return dest, own

    xs = [(x + i) % 4 for i in range(1, 4)]

    bar = pltpu.get_barrier_semaphore()

    def signal(d):
        pl.semaphore_signal(bar, inc=1, device_id=d, device_id_type=MESH)

    @pl.when(not_diag)
    def _():
        signal(mirror)

    for s in range(4):
        dest, own = leg2(s)

        @pl.when(jnp.logical_not(own))
        def _(dest=dest):
            signal(dest)

    ys = [(y1 * 2 + y0 + i) % 4 for i in range(1, 4)]
    for yy in ys:
        signal(device(x, yy // 2, yy % 2, z, c))
    for i in (1, 2, 6, 7):
        signal(device(x, y1, y0, (z + i) % 8, c))
    signal(sib)
    z_rel = x0 * 4 + y0 * 2 + z0
    for kk in range(4):

        @pl.when(jnp.logical_not((kk == x) & (z_rel == z)))
        def _(kk=kk):
            signal(device(kk, y1, y0, z_rel, c))

    for xx in xs:
        signal(device(xx, y1, y0, z, c))

    loads = [
        pltpu.make_async_copy(a, b, lsem.at[i])
        for i, (a, b) in enumerate(
            [(st_h, st), (wp_h, wp), (coef_h, coef), (wup_h, wup), (win_h.at[0], win.at[0]),
             (wout_h.at[0], wout.at[0]), (win_h.at[1], win.at[1]), (wout_h.at[1], wout.at[1])]
        )
    ]
    for cp in loads:
        cp.start()

    loads[0].wait()
    loads[1].wait()

    def proj_t(l, rows):
        return lax.dot_general(
            wp[l], rows, (((1,), (1,)), ((), ())), preferred_element_type=F32
        )

    def put_own(g, val):
        for b in range(4):
            g[me_slot * 4 + b] = val[:, b * BLK : (b + 1) * BLK].astype(BF16)

    put_own(g0, proj_t(0, st[...]))

    n_own2 = (y0 == z1).astype(jnp.int32)
    n_final = n_own2 * (8 - (x0 == z2).astype(jnp.int32))
    pl.semaphore_wait(bar, 8 + 3 + 4 - n_own2 + not_diag.astype(jnp.int32) + n_final)

    def remote(src, dst, ss, rs, d):
        return pltpu.make_async_remote_copy(
            src_ref=src, dst_ref=dst, send_sem=ss, recv_sem=rs, device_id=d, device_id_type=MESH
        )

    zup2 = device(x, y1, y0, (z + 2) % 8, c)
    zdn2 = device(x, y1, y0, (z + 6) % 8, c)

    def make_gather(l, g):
        def half(col, zz, h):
            return g.at[pl.ds((col * 16 + zz * 2 + c) * 4 + 2 * h, 2)]

        def origin(direction, dist):
            return (z + 8 - dist) % 8 if direction == 0 else (z + dist) % 8

        def to_sib(p):
            remote(p, p, gs.at[l], sr.at[l], sib).start()

        def z_copy(p, direction, dist, h):
            if dist == 4:
                d = zup2 if direction == 0 else zdn2
            else:
                d = zup if direction == 0 else zdn
            return remote(p, p, gs.at[l], zr.at[l, direction, dist - 1, h], d)

        def y_copy(p, direction, dist, h):
            i = dist if direction == 0 or dist == 0 else 4 + dist
            return remote(p, p, gs.at[l], yr.at[l, i, h], ypart)

        def ways(dist, h):
            return (0, 1) if dist < 4 else (h,)

        def start():
            for h in (0, 1):
                own = half(y1, z, h)
                for direction in (0, 1):
                    z_copy(own, direction, 1, h).start()
                y_copy(own, 0, 0, h).start()
                to_sib(own)

        def z_step(dist):
            for h in (0, 1):
                for direction in ways(dist, h):
                    got = half(y1, origin(direction, dist), h)
                    z_copy(got, direction, dist, h).wait_recv()
                    if dist < 3:
                        z_copy(got, direction, dist + 1, h).start()
                    if dist == 2 and direction == h:
                        z_copy(got, direction, 4, h).start()
                    y_copy(got, direction, dist, h).start()
                    to_sib(got)

        def y_step(dist):
            for h in (0, 1):
                for direction in ways(dist, h) if dist else (0,):
                    got = half(1 - y1, origin(direction, dist), h)
                    y_copy(got, direction, dist, h).wait_recv()
                    to_sib(got)

        def finish():
            all_sib = g.at[pl.ds(0, 64)]
            remote(all_sib, all_sib, gs.at[l], sr.at[l], sib).wait_recv()

        def drain():
            a = g.at[pl.ds(0, 4 * 31)]
            remote(a, a, gs.at[l], sr.at[l], sib).wait_send()

        return start, z_step, y_step, finish, drain

    gat0 = make_gather(0, g0)
    gat1 = make_gather(1, g1)
    gat0[0]()

    rows_sub = ROWS

    def sub(ref, slot, j):
        return ref.at[slot, pl.ds(j * rows_sub, rows_sub)]

    def st_sub(chunk, j):
        return st.at[pl.ds(chunk * BLK + j * rows_sub, rows_sub)]

    def fin_sub(chunk, j):
        return fin.at[pl.ds(chunk * BLK + j * rows_sub, rows_sub)]

    def leg1_start(j):
        for i, xx in enumerate(xs):
            remote(
                st_sub(xx, j), sub(l1, x, j), l1s.at[j], l1r.at[j, 3 - 1 - i], device(xx, y1, y0, z, c)
            ).start()

    def leg1_wait(j):
        for i, xx in enumerate(xs):
            remote(st_sub(xx, j), sub(l1, xx, j), l1s.at[j], l1r.at[j, i], sib).wait_recv()

    relay = y0 == z1

    def leg2_one(j, s, src):
        there = y1 * 2 + z2
        s1, s0 = s // 2, s % 2
        if j % 2:
            dest, own = leg2(s)

            @pl.when(jnp.logical_not(own))
            def _():
                remote(src, sub(l2, there, j), l2s.at[j], l2r.at[j, there], dest).start()

            @pl.when(own)
            def _():
                pltpu.make_async_copy(src, sub(l2, s, j), l2r.at[j, s]).start()

            return
        stays = relay & (y1 == s1)
        slot = (y1 * 2 + y0) * 2 + s0

        @pl.when(jnp.logical_not(stays))
        def _():
            remote(
                src, rel.at[j // 2, slot], l2as.at[j // 2], l2ar.at[j // 2, slot],
                device(x, s1, z1, z, c),
            ).start()

        @pl.when(stays)
        def _():
            pltpu.make_async_copy(src, rel.at[j // 2, slot], l2ar.at[j // 2, slot]).start()

    def leg2_own(j):
        leg2_one(j, x, st_sub(x, j))

    def leg2_start(j):
        for xx in xs:
            leg2_one(j, xx, sub(l1, xx, j))

    def leg2_relay(j):
        @pl.when(relay)
        def _():
            for ysrc in range(4):
                for s0 in range(2):
                    slot = ysrc * 2 + s0
                    here = rel.at[j // 2, slot]
                    t = (ysrc // 2) * 2 + z2
                    remote(here, here, l2as.at[j // 2], l2ar.at[j // 2, slot], sib).wait_recv()
                    stays = (z2 == s0) & (z1 == ysrc % 2) & (t == x)

                    @pl.when(jnp.logical_not(stays))
                    def _(here=here, t=t, s0=s0, ysrc=ysrc):
                        remote(
                            here, fin_sub(x, j), l2s.at[j], l3r.at[j, x],
                            device(t, y1, y0, s0 * 4 + (ysrc % 2) * 2 + z0, c),
                        ).start()

                    @pl.when(stays)
                    def _(here=here):
                        pltpu.make_async_copy(here, fin_sub(x, j), l3r.at[j, x]).start()

    def leg2_wait(j):
        for s in range(4):
            remote(sub(l1, s, j), sub(l2, s, j), l2s.at[j], l2r.at[j, s], sib).wait_recv()

    def leg3_start(j):
        for i, xx in enumerate(xs):
            remote(
                sub(l2, xx, j), fin_sub(x, j), l3s.at[j], l3r.at[j, x], device(xx, y1, y0, z, c)
            ).start()
        pltpu.make_async_copy(sub(l2, x, j), fin_sub(x, j), l3r.at[j, x]).start()

    def leg3_wait(j):
        for k in range(4):
            remote(sub(l2, k, j), fin_sub(k, j), l3s.at[j], l3r.at[j, k], sib).wait_recv()

    def legs_drain():
        rows = pl.ds(0, rows_sub)

        def gone(n, sem):
            ref = l1.at[pl.ds(0, n), rows] if n <= 4 else rel.at[0, pl.ds(0, n)]
            remote(ref, ref, sem, l1r.at[0, 0], sib).wait_send()

        for j in range(SUB):
            gone(3, l1s.at[j])
            if j % 2:
                gone(3, l3s.at[j])

            @pl.when(relay)
            def _(j=j):
                if j % 2:
                    gone(3, l2s.at[j])
                else:
                    gone(2, l2as.at[j // 2])

                    @pl.when(x0 == z2)
                    def _():
                        gone(7, l2s.at[j])

                    @pl.when(x0 != z2)
                    def _():
                        gone(8, l2s.at[j])

            @pl.when(jnp.logical_not(relay))
            def _(j=j):
                if j % 2:
                    gone(4, l2s.at[j])
                else:
                    gone(4, l2as.at[j // 2])

    def swap_start(i, src, dst):
        @pl.when(not_diag)
        def _():
            remote(src, dst, ms.at[i], mr.at[i], mirror).start()

        @pl.when(diag)
        def _():
            pltpu.make_async_copy(src, dst, mr.at[i]).start()

    def swap_wait(i, src, dst):
        @pl.when(not_diag)
        def _():
            remote(src, dst, ms.at[i], mr.at[i], mirror).wait_recv()

        @pl.when(diag)
        def _():
            pltpu.make_async_copy(src, dst, mr.at[i]).wait()

    def swap_drain(i, src, dst):
        @pl.when(not_diag)
        def _():
            remote(src, dst, ms.at[i], mr.at[i], mirror).wait_send()

    def triplets(g, out):
        live = cnt_s[0]
        zero = jnp.zeros((T, BLK), BF16)
        for b in range(NB):
            blk = g[src_s[b]]
            tb = jnp.where(b < live, tgt_s[b], -1)
            for o in range(4):
                lhs[o * T : (o + 1) * T, b * BLK : (b + 1) * BLK] = jnp.where(tb == o, blk, zero)
        acc = jnp.dot(lhs[...], coef[...].reshape(NB * BLK, BLK), preferred_element_type=F32)
        for o in range(4):
            out[:, o * BLK : (o + 1) * BLK] = acc[o * T : (o + 1) * T].astype(BF16)

    def permute_t(val):
        return jnp.dot(val, perm[...], preferred_element_type=F32)

    def layer_half(l, rows_ref, agg, sum_ref, br, r):
        def norm(i, _):
            rows = pl.ds(pl.multiple_of(r * 256 + i * BLK, BLK), BLK)
            up = lax.dot_general(
                agg[:, rows], wup[l], (((0,), (0,)), ((), ())), preferred_element_type=F32
            )
            s = rows_ref[rows, :].astype(F32) + up
            sum_ref[rows, :] = s
            scale = lax.rsqrt(jnp.mean(s * s, axis=-1, keepdims=True) + 1e-06)
            nrm[rows, :] = (gain_ref[l : l + 1, :] * s * scale).astype(BF16)
            return 0

        for i in range(2):
            norm(i, 0)
        rows = pl.ds(r * 256 if isinstance(r, int) else pl.multiple_of(r * 256, 256), 256)
        h = jnp.dot(nrm[rows, :], win[l], preferred_element_type=F32)
        h = 0.5 * h
        act[rows, :] = (h + h * jnp.tanh(h)).astype(BF16)
        br[rows, :] = jnp.dot(act[rows, :], wout[l], preferred_element_type=F32).astype(BF16)

    def layer(l, rows_ref, agg, sum_ref, br):
        def body(r, _):
            layer_half(l, rows_ref, agg, sum_ref, br, r)
            return 0

        lax.fori_loop(0, 2, body, 0)

    def by_rows(f):
        def body(r, _):
            f(pl.ds(pl.multiple_of(r * BLK, BLK), BLK))
            return 0

        lax.fori_loop(0, 4, body, 0)

    for j in range(SUB):
        leg1_start(j)

    def onehot(rows, r):
        ids = lax.broadcasted_iota(jnp.int32, (BLK, E), 0) + r * BLK
        perm[rows, :] = jnp.where(ids == rs_ref[0:1, :], 1.0, 0.0).astype(BF16)

    def onehot_body(r, _):
        onehot(pl.ds(pl.multiple_of(r * BLK, BLK), BLK), r)
        return 0

    lax.fori_loop(0, 4, onehot_body, 0)

    _, z_step, y_step, finish, drain0 = gat0
    z_step(1)
    leg2_own(0)
    leg2_own(1)
    y_step(0)
    leg1_wait(0)
    leg2_start(0)
    z_step(2)
    y_step(1)
    leg2_own(2)
    leg2_own(3)
    leg1_wait(1)
    leg2_start(1)
    z_step(3)
    z_step(4)
    y_step(2)
    leg1_wait(2)
    leg2_start(2)
    leg2_relay(0)
    y_step(3)
    leg1_wait(3)
    leg2_start(3)
    y_step(4)
    finish()

    loads[2].wait()
    triplets(g0, aggt.at[0])
    swap_start(0, aggt.at[0], aggm.at[0])
    leg2_relay(2)
    for i in (3, 4, 5):
        loads[i].wait()
    for r in (0, 1):
        rows = pl.ds(r * 256, 256)
        layer_half(0, st, aggt.at[0], summed, branch, r)
        pbt[r] = proj_t(1, branch[rows, :]).astype(BF16)
        swap_start(1 + r, pbt.at[r], pbm.at[r])
        if r == 0:
            leg2_wait(1)
            leg3_start(1)

    def part_sum(rows):
        nrm[rows, :] = (summed[rows, :] + branch[rows, :].astype(F32)).astype(BF16)

    by_rows(part_sum)
    half1 = proj_t(1, nrm[...])
    leg2_wait(3)
    leg3_start(3)
    swap_wait(1, pbt.at[0], pbm.at[0])
    swap_wait(2, pbt.at[1], pbm.at[1])
    mirrored_pb = jnp.dot(pbm[0], perm[0:256, :], preferred_element_type=F32) + jnp.dot(
        pbm[1], perm[256:512, :], preferred_element_type=F32
    )
    put_own(g1, half1 + mirrored_pb)
    start, z_step, y_step, finish, drain1 = gat1
    start()
    z_step(1)
    y_step(0)
    z_step(2)
    y_step(1)
    swap_wait(0, aggt.at[0], aggm.at[0])
    act[0:T, 0:E] = permute_t(aggm[0]).astype(BF16)
    aggm[0] = act[0:T, 0:E]
    z_step(3)
    z_step(4)
    y_step(2)

    for j in range(SUB):
        leg3_wait(j)

    def take_rows(r, _):
        rows = pl.ds(pl.multiple_of(r * 256, 256), 256)
        mst[rows, :] = lax.dot_general(
            perm[:, rows], fin[...], (((0,), (0,)), ((), ())), preferred_element_type=F32
        ).astype(BF16)
        return 0

    lax.fori_loop(0, 2, take_rows, 0)
    layer_half(0, mst, aggm.at[0], msum, mbr, 0)
    y_step(3)
    y_step(4)
    finish()
    triplets(g1, aggt.at[1])
    swap_start(3, aggt.at[1], aggm.at[1])
    layer_half(0, mst, aggm.at[0], msum, mbr, 1)

    def next_state(rows):
        b = branch[rows, :].astype(F32)
        m = mbr[rows, :].astype(F32)
        st[rows, :] = ((summed[rows, :] + b) + m).astype(BF16)
        mst[rows, :] = ((msum[rows, :] + m) + b).astype(BF16)

    legs_drain()
    by_rows(next_state)

    for i in (6, 7):
        loads[i].wait()
    layer(1, st, aggt.at[1], summed, branch)
    swap_wait(3, aggt.at[1], aggm.at[1])
    act[0:T, 0:E] = permute_t(aggm[1]).astype(BF16)
    aggm[1] = act[0:T, 0:E]
    layer(1, mst, aggm.at[1], msum, mbr)

    def final(rows):
        out_ref[rows, :] = (
            (summed[rows, :] + branch[rows, :].astype(F32)) + mbr[rows, :].astype(F32)
        ).astype(BF16)

    by_rows(final)

    drain0()
    drain1()
    swap_drain(0, aggt.at[0], aggm.at[0])
    swap_drain(1, pbt.at[0], pbm.at[0])
    swap_drain(2, pbt.at[1], pbm.at[1])
    swap_drain(3, aggt.at[1], aggm.at[1])


def local(
    edge_states, triplet_coeff, block_target, block_source, block_count, reverse_slot,
    w_proj, w_up, w_in, w_out, norm_gain,
):
    vmem = pl.BlockSpec(memory_space=pltpu.VMEM)
    smem = pl.BlockSpec(memory_space=pltpu.SMEM)
    hbm = pl.BlockSpec(memory_space=pltpu.HBM)
    dma = pltpu.SemaphoreType.DMA
    out = pl.pallas_call(
        kernel,
        out_shape=jax.ShapeDtypeStruct((E, D), BF16),
        in_specs=[smem, smem, smem, hbm, hbm, vmem, hbm, hbm, hbm, hbm, vmem],
        out_specs=vmem,
        scratch_shapes=[
            pltpu.VMEM((E, D), BF16),
            pltpu.VMEM((NB, BLK, BLK), BF16),
            pltpu.VMEM((2, T, D), BF16),
            pltpu.VMEM((2, T, D), BF16),
            pltpu.VMEM((2, D, D), BF16),
            pltpu.VMEM((2, D, D), BF16),
            pltpu.VMEM((NBLK, T, BLK), BF16),
            pltpu.VMEM((NBLK, T, BLK), BF16),
            pltpu.VMEM((4, BLK, D), BF16),
            pltpu.VMEM((4, BLK, D), BF16),
            pltpu.VMEM((SUB // 2, 8, ROWS, D), BF16),
            pltpu.VMEM((E, D), BF16),
            pltpu.VMEM((E, E), BF16),
            pltpu.VMEM((4 * T, NB * BLK), BF16),
            pltpu.VMEM((2, T, E), BF16),
            pltpu.VMEM((2, T, E), BF16),
            pltpu.VMEM((2, T, 256), BF16),
            pltpu.VMEM((2, T, 256), BF16),
            pltpu.VMEM((E, D), F32),
            pltpu.VMEM((E, D), BF16),
            pltpu.VMEM((E, D), BF16),
            pltpu.VMEM((E, D), F32),
            pltpu.VMEM((E, D), BF16),
            pltpu.VMEM((E, D), BF16),
            pltpu.VMEM((E, D), BF16),
            dma((8,)),
            dma((2,)),
            dma((2, 9, 2)),
            dma((2, 2, 4, 2)),
            dma((2,)),
            dma((SUB,)), dma((SUB, 4)),
            dma((SUB,)), dma((SUB, 4)),
            dma((SUB // 2,)), dma((SUB // 2, 8)),
            dma((SUB,)), dma((SUB, 4)),
            dma((4,)), dma((4,)),
        ],
        compiler_params=pltpu.CompilerParams(
            collective_id=0, has_side_effects=True, vmem_limit_bytes=56 << 20
        ),
        name="edge_layers",
    )(
        block_target[0, 0], block_source[0, 0], block_count[0], edge_states[0, 0],
        triplet_coeff[0, 0], reverse_slot[0], jnp.swapaxes(w_proj, 1, 2), w_up, w_in, w_out,
        norm_gain,
    )
    return out[None, None]


def solution(mesh):
    return jax.shard_map(
        local,
        mesh=mesh,
        in_specs=(
            P("src", "tgt", None, None),
            P("src", "tgt", None, None, None),
            P("src", "tgt", None),
            P("src", "tgt", None),
            P("src", "tgt"),
            P("src", "tgt", None),
            P(),
            P(),
            P(),
            P(),
            P(),
        ),
        out_specs=P("src", "tgt", None, None),
        check_vma=False,
    )
```

```python
import functools

import jax
import jax.numpy as jnp
from jax import lax
from jax.experimental import pallas as pl
from jax.experimental.pallas import tpu as pltpu
from jax.sharding import PartitionSpec as P

MESH = pl.DeviceIdType.MESH
BF16 = jnp.bfloat16
F32 = jnp.float32
D = 1024
E = 512
T = 64
BLK = 128
NB = 16
SUB = 8
ROWS = BLK // SUB
NBLK = 128


def place():
    s = lax.axis_index("src")
    t = lax.axis_index("tgt")
    return dict(y1=s // 16, z=(s // 2) % 8, c=s % 2, x=t // 2, y0=t % 2)


def device(x, y1, y0, z, c):
    return (y1 * 16 + z * 2 + c, x * 2 + y0)


def kernel(
    tgt_h, src_h, cnt_s, rs_h, gain_h, st_h, coef_h, wp_h, wup_h, win_h, wout_h, out_ref,
    tgt_s, src_s, rs_ref, gain_ref,
    st, coef, wp, wup, win, wout, g0, g1, l1, l2, rel, fin, perm, lhs, aggt, aggm, pbt, pbm,
    summed, branch, mst, msum, mbr, nrm, act, lsem,
    gs, yr, zr, sr, l1s, l1r, l2s, l2r, l2as, l2ar, l3s, l3r, ms, mr,
):
    k = place()
    x, y1, y0, z, c = k["x"], k["y1"], k["y0"], k["z"], k["c"]
    z2, z1, z0 = z // 4, (z // 2) % 2, z % 2
    x1, x0 = x // 2, x % 2
    me_slot = y1 * 16 + z * 2 + c

    sib = device(x, y1, y0, z, 1 - c)
    ypart = device(x, 1 - y1, y0, z, c)
    zup = device(x, y1, y0, (z + 1) % 8, c)
    zdn = device(x, y1, y0, (z + 7) % 8, c)
    mirror = device(y1 * 2 + z2, x1, z1, x0 * 4 + y0 * 2 + z0, c)
    diag = (x1 == y1) & (x0 == z2) & (y0 == z1)
    not_diag = jnp.logical_not(diag)

    def leg2(s):
        s1, s0 = s // 2, s % 2
        dest = device(x, s1, z1, s0 * 4 + y0 * 2 + z0, c)
        own = (y1 == s1) & (y0 == z1) & (z2 == s0)
        return dest, own

    xs = [(x + i) % 4 for i in range(1, 4)]

    bar = pltpu.get_barrier_semaphore()

    def signal(d):
        pl.semaphore_signal(bar, inc=1, device_id=d, device_id_type=MESH)

    @pl.when(not_diag)
    def _():
        signal(mirror)

    for s in range(4):
        dest, own = leg2(s)

        @pl.when(jnp.logical_not(own))
        def _(dest=dest):
            signal(dest)

    ys = [(y1 * 2 + y0 + i) % 4 for i in range(1, 4)]
    for yy in ys:
        signal(device(x, yy // 2, yy % 2, z, c))
    for i in (1, 2, 6, 7):
        signal(device(x, y1, y0, (z + i) % 8, c))
    signal(sib)
    z_rel = x0 * 4 + y0 * 2 + z0
    for kk in range(4):

        @pl.when(jnp.logical_not((kk == x) & (z_rel == z)))
        def _(kk=kk):
            signal(device(kk, y1, y0, z_rel, c))

    for xx in xs:
        signal(device(xx, y1, y0, z, c))

    loads = [
        pltpu.make_async_copy(a, b, lsem.at[i])
        for i, (a, b) in enumerate(
            [(st_h, st), (wp_h, wp), (coef_h, coef), (wup_h, wup), (win_h.at[0], win.at[0]),
             (wout_h.at[0], wout.at[0]), (win_h.at[1], win.at[1]), (wout_h.at[1], wout.at[1]),
             (rs_h, rs_ref), (gain_h, gain_ref), (tgt_h, tgt_s), (src_h, src_s)]
        )
    ]
    for cp in loads:
        cp.start()

    loads[0].wait()
    loads[1].wait()

    def proj_t(l, rows):
        return lax.dot_general(
            wp[l], rows, (((1,), (1,)), ((), ())), preferred_element_type=F32
        )

    def put_own(g, val):
        for b in range(4):
            g[me_slot * 4 + b] = val[:, b * BLK : (b + 1) * BLK].astype(BF16)

    put_own(g0, proj_t(0, st[...]))

    n_own2 = (y0 == z1).astype(jnp.int32)
    n_final = n_own2 * (8 - (x0 == z2).astype(jnp.int32))
    pl.semaphore_wait(bar, 8 + 3 + 4 - n_own2 + not_diag.astype(jnp.int32) + n_final)

    def remote(src, dst, ss, rs, d):
        return pltpu.make_async_remote_copy(
            src_ref=src, dst_ref=dst, send_sem=ss, recv_sem=rs, device_id=d, device_id_type=MESH
        )

    zup2 = device(x, y1, y0, (z + 2) % 8, c)
    zdn2 = device(x, y1, y0, (z + 6) % 8, c)

    def make_gather(l, g):
        def half(col, zz, h):
            return g.at[pl.ds((col * 16 + zz * 2 + c) * 4 + 2 * h, 2)]

        def origin(direction, dist):
            return (z + 8 - dist) % 8 if direction == 0 else (z + dist) % 8

        def to_sib(p):
            remote(p, p, gs.at[l], sr.at[l], sib).start()

        def z_copy(p, direction, dist, h):
            if dist == 4:
                d = zup2 if direction == 0 else zdn2
            else:
                d = zup if direction == 0 else zdn
            return remote(p, p, gs.at[l], zr.at[l, direction, dist - 1, h], d)

        def y_copy(p, direction, dist, h):
            i = dist if direction == 0 or dist == 0 else 4 + dist
            return remote(p, p, gs.at[l], yr.at[l, i, h], ypart)

        def ways(dist, h):
            return (0, 1) if dist < 4 else (h,)

        def start():
            for h in (0, 1):
                own = half(y1, z, h)
                for direction in (0, 1):
                    z_copy(own, direction, 1, h).start()
                y_copy(own, 0, 0, h).start()
                to_sib(own)

        def z_step(dist):
            for h in (0, 1):
                for direction in ways(dist, h):
                    got = half(y1, origin(direction, dist), h)
                    z_copy(got, direction, dist, h).wait_recv()
                    if dist < 3:
                        z_copy(got, direction, dist + 1, h).start()
                    if dist == 2 and direction == h:
                        z_copy(got, direction, 4, h).start()
                    y_copy(got, direction, dist, h).start()
                    to_sib(got)

        def y_step(dist):
            for h in (0, 1):
                for direction in ways(dist, h) if dist else (0,):
                    got = half(1 - y1, origin(direction, dist), h)
                    y_copy(got, direction, dist, h).wait_recv()
                    to_sib(got)

        def finish():
            all_sib = g.at[pl.ds(0, 64)]
            remote(all_sib, all_sib, gs.at[l], sr.at[l], sib).wait_recv()

        def drain():
            a = g.at[pl.ds(0, 4 * 31)]
            remote(a, a, gs.at[l], sr.at[l], sib).wait_send()

        return start, z_step, y_step, finish, drain

    gat0 = make_gather(0, g0)
    gat1 = make_gather(1, g1)
    gat0[0]()

    rows_sub = ROWS

    def sub(ref, slot, j):
        return ref.at[slot, pl.ds(j * rows_sub, rows_sub)]

    def st_sub(chunk, j):
        return st.at[pl.ds(chunk * BLK + j * rows_sub, rows_sub)]

    def fin_sub(chunk, j):
        return fin.at[pl.ds(chunk * BLK + j * rows_sub, rows_sub)]

    def leg1_start(j):
        for i, xx in enumerate(xs):
            remote(
                st_sub(xx, j), sub(l1, x, j), l1s.at[j], l1r.at[j, 3 - 1 - i], device(xx, y1, y0, z, c)
            ).start()

    def leg1_wait(j):
        for i, xx in enumerate(xs):
            remote(st_sub(xx, j), sub(l1, xx, j), l1s.at[j], l1r.at[j, i], sib).wait_recv()

    relay = y0 == z1

    def leg2_one(j, s, src):
        there = y1 * 2 + z2
        s1, s0 = s // 2, s % 2
        if j % 2:
            dest, own = leg2(s)

            @pl.when(jnp.logical_not(own))
            def _():
                remote(src, sub(l2, there, j), l2s.at[j], l2r.at[j, there], dest).start()

            @pl.when(own)
            def _():
                pltpu.make_async_copy(src, sub(l2, s, j), l2r.at[j, s]).start()

            return
        stays = relay & (y1 == s1)
        slot = (y1 * 2 + y0) * 2 + s0

        @pl.when(jnp.logical_not(stays))
        def _():
            remote(
                src, rel.at[j // 2, slot], l2as.at[j // 2], l2ar.at[j // 2, slot],
                device(x, s1, z1, z, c),
            ).start()

        @pl.when(stays)
        def _():
            pltpu.make_async_copy(src, rel.at[j // 2, slot], l2ar.at[j // 2, slot]).start()

    def leg2_own(j):
        leg2_one(j, x, st_sub(x, j))

    def leg2_start(j):
        for xx in xs:
            leg2_one(j, xx, sub(l1, xx, j))

    def leg2_relay(j):
        @pl.when(relay)
        def _():
            for ysrc in range(4):
                for s0 in range(2):
                    slot = ysrc * 2 + s0
                    here = rel.at[j // 2, slot]
                    t = (ysrc // 2) * 2 + z2
                    remote(here, here, l2as.at[j // 2], l2ar.at[j // 2, slot], sib).wait_recv()
                    stays = (z2 == s0) & (z1 == ysrc % 2) & (t == x)

                    @pl.when(jnp.logical_not(stays))
                    def _(here=here, t=t, s0=s0, ysrc=ysrc):
                        remote(
                            here, fin_sub(x, j), l2s.at[j], l3r.at[j, x],
                            device(t, y1, y0, s0 * 4 + (ysrc % 2) * 2 + z0, c),
                        ).start()

                    @pl.when(stays)
                    def _(here=here):
                        pltpu.make_async_copy(here, fin_sub(x, j), l3r.at[j, x]).start()

    def leg2_wait(j):
        for s in range(4):
            remote(sub(l1, s, j), sub(l2, s, j), l2s.at[j], l2r.at[j, s], sib).wait_recv()

    def leg3_start(j):
        for i, xx in enumerate(xs):
            remote(
                sub(l2, xx, j), fin_sub(x, j), l3s.at[j], l3r.at[j, x], device(xx, y1, y0, z, c)
            ).start()
        pltpu.make_async_copy(sub(l2, x, j), fin_sub(x, j), l3r.at[j, x]).start()

    def leg3_wait(j):
        for k in range(4):
            remote(sub(l2, k, j), fin_sub(k, j), l3s.at[j], l3r.at[j, k], sib).wait_recv()

    def legs_drain():
        rows = pl.ds(0, rows_sub)

        def gone(n, sem):
            ref = l1.at[pl.ds(0, n), rows] if n <= 4 else rel.at[0, pl.ds(0, n)]
            remote(ref, ref, sem, l1r.at[0, 0], sib).wait_send()

        for j in range(SUB):
            gone(3, l1s.at[j])
            if j % 2:
                gone(3, l3s.at[j])

            @pl.when(relay)
            def _(j=j):
                if j % 2:
                    gone(3, l2s.at[j])
                else:
                    gone(2, l2as.at[j // 2])

                    @pl.when(x0 == z2)
                    def _():
                        gone(7, l2s.at[j])

                    @pl.when(x0 != z2)
                    def _():
                        gone(8, l2s.at[j])

            @pl.when(jnp.logical_not(relay))
            def _(j=j):
                if j % 2:
                    gone(4, l2s.at[j])
                else:
                    gone(4, l2as.at[j // 2])

    def swap_start(i, src, dst):
        @pl.when(not_diag)
        def _():
            remote(src, dst, ms.at[i], mr.at[i], mirror).start()

        @pl.when(diag)
        def _():
            pltpu.make_async_copy(src, dst, mr.at[i]).start()

    def swap_wait(i, src, dst):
        @pl.when(not_diag)
        def _():
            remote(src, dst, ms.at[i], mr.at[i], mirror).wait_recv()

        @pl.when(diag)
        def _():
            pltpu.make_async_copy(src, dst, mr.at[i]).wait()

    def swap_drain(i, src, dst):
        @pl.when(not_diag)
        def _():
            remote(src, dst, ms.at[i], mr.at[i], mirror).wait_send()

    def triplets(g, out):
        live = cnt_s[0]
        zero = jnp.zeros((T, BLK), BF16)
        for b in range(NB):
            blk = g[src_s[b]]
            tb = jnp.where(b < live, tgt_s[b], -1)
            for o in range(4):
                lhs[o * T : (o + 1) * T, b * BLK : (b + 1) * BLK] = jnp.where(tb == o, blk, zero)
        acc = jnp.dot(lhs[...], coef[...].reshape(NB * BLK, BLK), preferred_element_type=F32)
        for o in range(4):
            out[:, o * BLK : (o + 1) * BLK] = acc[o * T : (o + 1) * T].astype(BF16)

    def permute_t(val):
        return jnp.dot(val, perm[...], preferred_element_type=F32)

    def layer_half(l, rows_ref, agg, sum_ref, br, r):
        def norm(i, _):
            rows = pl.ds(pl.multiple_of(r * 256 + i * BLK, BLK), BLK)
            up = lax.dot_general(
                agg[:, rows], wup[l], (((0,), (0,)), ((), ())), preferred_element_type=F32
            )
            s = rows_ref[rows, :].astype(F32) + up
            if sum_ref is not None:
                sum_ref[rows, :] = s
            scale = lax.rsqrt(jnp.mean(s * s, axis=-1, keepdims=True) + 1e-06)
            nrm[rows, :] = (gain_ref[l : l + 1, :] * s * scale).astype(BF16)
            return 0

        for i in range(2):
            norm(i, 0)
        rows = pl.ds(r * 256 if isinstance(r, int) else pl.multiple_of(r * 256, 256), 256)
        h = jnp.dot(nrm[rows, :], win[l], preferred_element_type=F32)
        h = 0.5 * h
        act[rows, :] = (h + h * jnp.tanh(h)).astype(BF16)
        val = jnp.dot(act[rows, :], wout[l], preferred_element_type=F32).astype(BF16)
        if br is None:
            out_ref[rows, :] = (
                (summed[rows, :] + branch[rows, :].astype(F32)) + val.astype(F32)
            ).astype(BF16)
        else:
            br[rows, :] = val

    def layer(l, rows_ref, agg, sum_ref, br):
        for r in (0, 1):
            layer_half(l, rows_ref, agg, sum_ref, br, r)

    def by_rows(f):
        def body(r, _):
            f(pl.ds(pl.multiple_of(r * BLK, BLK), BLK))
            return 0

        lax.fori_loop(0, 4, body, 0)

    for j in range(SUB):
        leg1_start(j)

    for i in range(8, 12):
        loads[i].wait()

    def onehot(rows, r):
        ids = lax.broadcasted_iota(jnp.int32, (BLK, E), 0) + r * BLK
        perm[rows, :] = jnp.where(ids == rs_ref[0:1, :], 1.0, 0.0).astype(BF16)

    def onehot_body(r, _):
        onehot(pl.ds(pl.multiple_of(r * BLK, BLK), BLK), r)
        return 0

    lax.fori_loop(0, 4, onehot_body, 0)

    _, z_step, y_step, finish, drain0 = gat0
    z_step(1)
    leg2_own(0)
    leg2_own(1)
    y_step(0)
    leg1_wait(0)
    leg2_start(0)
    leg2_own(2)
    leg2_own(3)
    z_step(2)
    leg1_wait(1)
    leg2_start(1)
    y_step(1)
    leg1_wait(2)
    leg2_start(2)
    leg2_own(4)
    leg2_own(5)
    leg1_wait(3)
    leg2_start(3)
    z_step(3)
    leg2_own(6)
    leg2_own(7)
    z_step(4)
    leg1_wait(4)
    leg2_start(4)
    y_step(2)
    leg2_relay(0)
    leg1_wait(5)
    leg2_start(5)
    y_step(3)
    leg1_wait(6)
    leg2_start(6)
    leg2_relay(2)
    leg1_wait(7)
    leg2_start(7)
    y_step(4)
    finish()
    loads[2].wait()
    triplets(g0, aggt.at[0])
    swap_start(0, aggt.at[0], aggm.at[0])
    leg2_relay(4)
    for i in (3, 4, 5):
        loads[i].wait()
    for r in (0, 1):
        rows = pl.ds(r * 256, 256)
        layer_half(0, st, aggt.at[0], summed, branch, r)
        pbt[r] = proj_t(1, branch[rows, :]).astype(BF16)
        swap_start(1 + r, pbt.at[r], pbm.at[r])
        if r == 0:
            leg2_wait(1)
            leg3_start(1)
            leg2_wait(3)
            leg3_start(3)

    def part_sum(rows):
        nrm[rows, :] = (summed[rows, :] + branch[rows, :].astype(F32)).astype(BF16)

    by_rows(part_sum)
    half1 = proj_t(1, nrm[...])
    leg2_relay(6)
    leg2_wait(5)
    leg3_start(5)
    leg2_wait(7)
    leg3_start(7)
    swap_wait(1, pbt.at[0], pbm.at[0])
    swap_wait(2, pbt.at[1], pbm.at[1])
    mirrored_pb = jnp.dot(pbm[0], perm[0:256, :], preferred_element_type=F32) + jnp.dot(
        pbm[1], perm[256:512, :], preferred_element_type=F32
    )
    put_own(g1, half1 + mirrored_pb)
    start, z_step, y_step, finish, drain1 = gat1
    start()
    z_step(1)
    y_step(0)
    z_step(2)
    y_step(1)
    swap_wait(0, aggt.at[0], aggm.at[0])
    act[0:T, 0:E] = permute_t(aggm[0]).astype(BF16)
    aggm[0] = act[0:T, 0:E]
    z_step(3)
    z_step(4)
    y_step(2)
    for j in range(SUB):
        leg3_wait(j)

    def take_rows(r, _):
        rows = pl.ds(pl.multiple_of(r * 256, 256), 256)
        mst[rows, :] = lax.dot_general(
            perm[:, rows], fin[...], (((0,), (0,)), ((), ())), preferred_element_type=F32
        ).astype(BF16)
        return 0

    lax.fori_loop(0, 2, take_rows, 0)
    layer_half(0, mst, aggm.at[0], msum, mbr, 0)
    y_step(3)
    y_step(4)
    finish()
    triplets(g1, aggt.at[1])
    swap_start(3, aggt.at[1], aggm.at[1])
    layer_half(0, mst, aggm.at[0], msum, mbr, 1)

    def next_state(rows):
        b = branch[rows, :].astype(F32)
        m = mbr[rows, :].astype(F32)
        st[rows, :] = ((summed[rows, :] + b) + m).astype(BF16)
        mst[rows, :] = ((msum[rows, :] + m) + b).astype(BF16)

    legs_drain()
    by_rows(next_state)

    for i in (6, 7):
        loads[i].wait()
    layer(1, st, aggt.at[1], summed, branch)
    swap_wait(3, aggt.at[1], aggm.at[1])
    act[0:T, 0:E] = permute_t(aggm[1]).astype(BF16)
    aggm[1] = act[0:T, 0:E]
    layer(1, mst, aggm.at[1], None, None)

    drain0()
    drain1()
    swap_drain(0, aggt.at[0], aggm.at[0])
    swap_drain(1, pbt.at[0], pbm.at[0])
    swap_drain(2, pbt.at[1], pbm.at[1])
    swap_drain(3, aggt.at[1], aggm.at[1])


def local(
    edge_states, triplet_coeff, block_target, block_source, block_count, reverse_slot,
    w_proj, w_up, w_in, w_out, norm_gain,
):
    vmem = pl.BlockSpec(memory_space=pltpu.VMEM)
    smem = pl.BlockSpec(memory_space=pltpu.SMEM)
    hbm = pl.BlockSpec(memory_space=pltpu.HBM)
    dma = pltpu.SemaphoreType.DMA
    def stay(a):
        return pltpu.with_memory_space_constraint(a, pltpu.HBM)

    out = pl.pallas_call(
        kernel,
        out_shape=jax.ShapeDtypeStruct((E, D), BF16),
        in_specs=[hbm, hbm, smem] + [hbm] * 8,
        out_specs=vmem,
        scratch_shapes=[
            pltpu.SMEM((NB,), jnp.int32),
            pltpu.SMEM((NB,), jnp.int32),
            pltpu.VMEM((1, E), jnp.int32),
            pltpu.VMEM((2, D), F32),
            pltpu.VMEM((E, D), BF16),
            pltpu.VMEM((NB, BLK, BLK), BF16),
            pltpu.VMEM((2, T, D), BF16),
            pltpu.VMEM((2, T, D), BF16),
            pltpu.VMEM((2, D, D), BF16),
            pltpu.VMEM((2, D, D), BF16),
            pltpu.VMEM((NBLK, T, BLK), BF16),
            pltpu.VMEM((NBLK, T, BLK), BF16),
            pltpu.VMEM((4, BLK, D), BF16),
            pltpu.VMEM((4, BLK, D), BF16),
            pltpu.VMEM((SUB // 2, 8, ROWS, D), BF16),
            pltpu.VMEM((E, D), BF16),
            pltpu.VMEM((E, E), BF16),
            pltpu.VMEM((4 * T, NB * BLK), BF16),
            pltpu.VMEM((2, T, E), BF16),
            pltpu.VMEM((2, T, E), BF16),
            pltpu.VMEM((2, T, 256), BF16),
            pltpu.VMEM((2, T, 256), BF16),
            pltpu.VMEM((E, D), F32),
            pltpu.VMEM((E, D), BF16),
            pltpu.VMEM((E, D), BF16),
            pltpu.VMEM((E, D), F32),
            pltpu.VMEM((E, D), BF16),
            pltpu.VMEM((E, D), BF16),
            pltpu.VMEM((E, D), BF16),
            dma((12,)),
            dma((2,)),
            dma((2, 9, 2)),
            dma((2, 2, 4, 2)),
            dma((2,)),
            dma((SUB,)), dma((SUB, 4)),
            dma((SUB,)), dma((SUB, 4)),
            dma((SUB // 2,)), dma((SUB // 2, 8)),
            dma((SUB,)), dma((SUB, 4)),
            dma((4,)), dma((4,)),
        ],
        compiler_params=pltpu.CompilerParams(
            collective_id=0, has_side_effects=True, vmem_limit_bytes=48 << 20
        ),
        name="edge_layers",
    )(
        *map(stay, (block_target[0, 0], block_source[0, 0])),
        block_count[0],
        *map(
            stay,
            (
                reverse_slot[0], norm_gain, edge_states[0, 0], triplet_coeff[0, 0],
                jnp.swapaxes(w_proj, 1, 2), w_up, w_in, w_out,
            ),
        ),
    )
    return out[None, None]


def solution(mesh):
    return jax.shard_map(
        local,
        mesh=mesh,
        in_specs=(
            P("src", "tgt", None, None),
            P("src", "tgt", None, None, None),
            P("src", "tgt", None),
            P("src", "tgt", None),
            P("src", "tgt"),
            P("src", "tgt", None),
            P(),
            P(),
            P(),
            P(),
            P(),
        ),
        out_specs=P("src", "tgt", None, None),
        check_vma=False,
    )
```

```python
import functools

import jax
import jax.numpy as jnp
from jax import lax
from jax.experimental import pallas as pl
from jax.experimental.pallas import tpu as pltpu
from jax.sharding import PartitionSpec as P

MESH = pl.DeviceIdType.MESH
BF16 = jnp.bfloat16
F32 = jnp.float32
D = 1024
E = 512
T = 64
BLK = 128
NB = 16
SUB = 8
ROWS = BLK // SUB
NBLK = 128


def place():
    s = lax.axis_index("src")
    t = lax.axis_index("tgt")
    return dict(y1=s // 16, z=(s // 2) % 8, c=s % 2, x=t // 2, y0=t % 2)


def device(x, y1, y0, z, c):
    return (y1 * 16 + z * 2 + c, x * 2 + y0)


def kernel(
    tgt_h, src_h, cnt_s, rs_h, gain_h, st_h, coef_h, wp_h, wup_h, win_h, wout_h, out_ref,
    tgt_s, src_s, rs_ref, gain_ref,
    st, coef, wp, wup, win, wout, g0, g1, l1, l2, rel, fin, perm, lhs, aggt, aggm, pbt, pbm,
    summed, branch, mst, msum, mbr, nrm, act, lsem,
    gs, yr, zr, sr, l1s, l1r, l2s, l2r, l2as, l2ar, l3s, l3r, ms, mr,
):
    k = place()
    x, y1, y0, z, c = k["x"], k["y1"], k["y0"], k["z"], k["c"]
    z2, z1, z0 = z // 4, (z // 2) % 2, z % 2
    x1, x0 = x // 2, x % 2
    me_slot = y1 * 16 + z * 2 + c

    sib = device(x, y1, y0, z, 1 - c)
    ypart = device(x, 1 - y1, y0, z, c)
    zup = device(x, y1, y0, (z + 1) % 8, c)
    zdn = device(x, y1, y0, (z + 7) % 8, c)
    mirror = device(y1 * 2 + z2, x1, z1, x0 * 4 + y0 * 2 + z0, c)
    diag = (x1 == y1) & (x0 == z2) & (y0 == z1)
    not_diag = jnp.logical_not(diag)

    def leg2(s):
        s1, s0 = s // 2, s % 2
        dest = device(x, s1, z1, s0 * 4 + y0 * 2 + z0, c)
        own = (y1 == s1) & (y0 == z1) & (z2 == s0)
        return dest, own

    xs = [(x + i) % 4 for i in range(1, 4)]

    bar = pltpu.get_barrier_semaphore()

    def signal(d):
        pl.semaphore_signal(bar, inc=1, device_id=d, device_id_type=MESH)

    @pl.when(not_diag)
    def _():
        signal(mirror)

    for s in range(4):
        dest, own = leg2(s)

        @pl.when(jnp.logical_not(own))
        def _(dest=dest):
            signal(dest)

    ys = [(y1 * 2 + y0 + i) % 4 for i in range(1, 4)]
    for yy in ys:
        signal(device(x, yy // 2, yy % 2, z, c))
    for i in (1, 2, 6, 7):
        signal(device(x, y1, y0, (z + i) % 8, c))
    signal(sib)
    z_rel = x0 * 4 + y0 * 2 + z0
    for kk in range(4):

        @pl.when(jnp.logical_not((kk == x) & (z_rel == z)))
        def _(kk=kk):
            signal(device(kk, y1, y0, z_rel, c))

    for xx in xs:
        signal(device(xx, y1, y0, z, c))

    loads = [
        pltpu.make_async_copy(a, b, lsem.at[i])
        for i, (a, b) in enumerate(
            [(st_h, st), (wp_h, wp), (coef_h, coef), (wup_h, wup), (win_h.at[0], win.at[0]),
             (wout_h.at[0], wout.at[0]), (win_h.at[1], win.at[1]), (wout_h.at[1], wout.at[1]),
             (rs_h, rs_ref), (gain_h, gain_ref), (tgt_h, tgt_s), (src_h, src_s)]
        )
    ]
    for cp in loads:
        cp.start()

    loads[0].wait()
    loads[1].wait()

    def proj_t(l, rows):
        return lax.dot_general(
            wp[l], rows, (((1,), (1,)), ((), ())), preferred_element_type=F32
        )

    def put_own(g, val):
        for b in range(4):
            g[me_slot * 4 + b] = val[:, b * BLK : (b + 1) * BLK].astype(BF16)

    put_own(g0, proj_t(0, st[...]))

    n_own2 = (y0 == z1).astype(jnp.int32)
    n_final = n_own2 * (8 - (x0 == z2).astype(jnp.int32))
    pl.semaphore_wait(bar, 8 + 3 + 4 - n_own2 + not_diag.astype(jnp.int32) + n_final)

    def remote(src, dst, ss, rs, d):
        return pltpu.make_async_remote_copy(
            src_ref=src, dst_ref=dst, send_sem=ss, recv_sem=rs, device_id=d, device_id_type=MESH
        )

    zup2 = device(x, y1, y0, (z + 2) % 8, c)
    zdn2 = device(x, y1, y0, (z + 6) % 8, c)

    def make_gather(l, g):
        def half(col, zz, h):
            return g.at[pl.ds((col * 16 + zz * 2 + c) * 4 + 2 * h, 2)]

        def origin(direction, dist):
            return (z + 8 - dist) % 8 if direction == 0 else (z + dist) % 8

        def to_sib(p):
            remote(p, p, gs.at[l], sr.at[l], sib).start()

        def z_copy(p, direction, dist, h):
            if dist == 4:
                d = zup2 if direction == 0 else zdn2
            else:
                d = zup if direction == 0 else zdn
            return remote(p, p, gs.at[l], zr.at[l, direction, dist - 1, h], d)

        def y_copy(p, direction, dist, h):
            i = dist if direction == 0 or dist == 0 else 4 + dist
            return remote(p, p, gs.at[l], yr.at[l, i, h], ypart)

        def ways(dist, h):
            return (0, 1) if dist < 4 else (h,)

        def start():
            for h in (0, 1):
                for direction in (0, 1):
                    z_copy(half(y1, z, h), direction, 1, h).start()
            for h in (0, 1):
                y_copy(half(y1, z, h), 0, 0, h).start()
            for h in (0, 1):
                to_sib(half(y1, z, h))

        def z_step(dist):
            for h in (0, 1):
                for direction in ways(dist, h):
                    got = half(y1, origin(direction, dist), h)
                    z_copy(got, direction, dist, h).wait_recv()
                    if dist < 3:
                        z_copy(got, direction, dist + 1, h).start()
                    if dist == 2 and direction == h:
                        z_copy(got, direction, 4, h).start()
                for direction in ways(dist, h):
                    y_copy(half(y1, origin(direction, dist), h), direction, dist, h).start()
                for direction in ways(dist, h):
                    to_sib(half(y1, origin(direction, dist), h))

        def y_step(dist):
            for h in (0, 1):
                for direction in ways(dist, h) if dist else (0,):
                    got = half(1 - y1, origin(direction, dist), h)
                    y_copy(got, direction, dist, h).wait_recv()
                    to_sib(got)

        def finish():
            all_sib = g.at[pl.ds(0, 64)]
            remote(all_sib, all_sib, gs.at[l], sr.at[l], sib).wait_recv()

        def drain():
            a = g.at[pl.ds(0, 4 * 31)]
            remote(a, a, gs.at[l], sr.at[l], sib).wait_send()

        return start, z_step, y_step, finish, drain

    gat0 = make_gather(0, g0)
    gat1 = make_gather(1, g1)
    gat0[0]()

    rows_sub = ROWS

    def sub(ref, slot, j):
        return ref.at[slot, pl.ds(j * rows_sub, rows_sub)]

    def st_sub(chunk, j):
        return st.at[pl.ds(chunk * BLK + j * rows_sub, rows_sub)]

    def fin_sub(chunk, j):
        return fin.at[pl.ds(chunk * BLK + j * rows_sub, rows_sub)]

    def leg1_start(j):
        for i, xx in enumerate(xs):
            remote(
                st_sub(xx, j), sub(l1, x, j), l1s.at[j], l1r.at[j, 3 - 1 - i], device(xx, y1, y0, z, c)
            ).start()

    def leg1_wait(j):
        for i, xx in enumerate(xs):
            remote(st_sub(xx, j), sub(l1, xx, j), l1s.at[j], l1r.at[j, i], sib).wait_recv()

    relay = y0 == z1

    def leg2_one(j, s, src):
        there = y1 * 2 + z2
        s1, s0 = s // 2, s % 2
        if j % 2:
            dest, own = leg2(s)

            @pl.when(jnp.logical_not(own))
            def _():
                remote(src, sub(l2, there, j), l2s.at[j], l2r.at[j, there], dest).start()

            @pl.when(own)
            def _():
                pltpu.make_async_copy(src, sub(l2, s, j), l2r.at[j, s]).start()

            return
        stays = relay & (y1 == s1)
        slot = (y1 * 2 + y0) * 2 + s0

        @pl.when(jnp.logical_not(stays))
        def _():
            remote(
                src, rel.at[j // 2, slot], l2as.at[j // 2], l2ar.at[j // 2, slot],
                device(x, s1, z1, z, c),
            ).start()

        @pl.when(stays)
        def _():
            pltpu.make_async_copy(src, rel.at[j // 2, slot], l2ar.at[j // 2, slot]).start()

    def leg2_own(j):
        leg2_one(j, x, st_sub(x, j))

    def leg2_start(j):
        for xx in xs:
            leg2_one(j, xx, sub(l1, xx, j))

    def leg2_relay(j):
        @pl.when(relay)
        def _():
            for ysrc in range(4):
                for s0 in range(2):
                    slot = ysrc * 2 + s0
                    here = rel.at[j // 2, slot]
                    t = (ysrc // 2) * 2 + z2
                    remote(here, here, l2as.at[j // 2], l2ar.at[j // 2, slot], sib).wait_recv()
                    stays = (z2 == s0) & (z1 == ysrc % 2) & (t == x)

                    @pl.when(jnp.logical_not(stays))
                    def _(here=here, t=t, s0=s0, ysrc=ysrc):
                        remote(
                            here, fin_sub(x, j), l2s.at[j], l3r.at[j, x],
                            device(t, y1, y0, s0 * 4 + (ysrc % 2) * 2 + z0, c),
                        ).start()

                    @pl.when(stays)
                    def _(here=here):
                        pltpu.make_async_copy(here, fin_sub(x, j), l3r.at[j, x]).start()

    def leg2_wait(j):
        for s in range(4):
            remote(sub(l1, s, j), sub(l2, s, j), l2s.at[j], l2r.at[j, s], sib).wait_recv()

    def leg3_start(j):
        for i, xx in enumerate(xs):
            remote(
                sub(l2, xx, j), fin_sub(x, j), l3s.at[j], l3r.at[j, x], device(xx, y1, y0, z, c)
            ).start()
        pltpu.make_async_copy(sub(l2, x, j), fin_sub(x, j), l3r.at[j, x]).start()

    def leg3_wait(j):
        for k in range(4):
            remote(sub(l2, k, j), fin_sub(k, j), l3s.at[j], l3r.at[j, k], sib).wait_recv()

    def legs_drain():
        rows = pl.ds(0, rows_sub)

        def gone(n, sem):
            ref = l1.at[pl.ds(0, n), rows] if n <= 4 else rel.at[0, pl.ds(0, n)]
            remote(ref, ref, sem, l1r.at[0, 0], sib).wait_send()

        for j in range(SUB):
            gone(3, l1s.at[j])
            if j % 2:
                gone(3, l3s.at[j])

            @pl.when(relay)
            def _(j=j):
                if j % 2:
                    gone(3, l2s.at[j])
                else:
                    gone(2, l2as.at[j // 2])

                    @pl.when(x0 == z2)
                    def _():
                        gone(7, l2s.at[j])

                    @pl.when(x0 != z2)
                    def _():
                        gone(8, l2s.at[j])

            @pl.when(jnp.logical_not(relay))
            def _(j=j):
                if j % 2:
                    gone(4, l2s.at[j])
                else:
                    gone(4, l2as.at[j // 2])

    def swap_start(i, src, dst):
        @pl.when(not_diag)
        def _():
            remote(src, dst, ms.at[i], mr.at[i], mirror).start()

        @pl.when(diag)
        def _():
            pltpu.make_async_copy(src, dst, mr.at[i]).start()

    def swap_wait(i, src, dst):
        @pl.when(not_diag)
        def _():
            remote(src, dst, ms.at[i], mr.at[i], mirror).wait_recv()

        @pl.when(diag)
        def _():
            pltpu.make_async_copy(src, dst, mr.at[i]).wait()

    def swap_drain(i, src, dst):
        @pl.when(not_diag)
        def _():
            remote(src, dst, ms.at[i], mr.at[i], mirror).wait_send()

    def triplets(g, out):
        live = cnt_s[0]
        zero = jnp.zeros((T, BLK), BF16)
        for b in range(NB):
            blk = g[src_s[b]]
            tb = jnp.where(b < live, tgt_s[b], -1)
            for o in range(4):
                lhs[o * T : (o + 1) * T, b * BLK : (b + 1) * BLK] = jnp.where(tb == o, blk, zero)
        acc = jnp.dot(lhs[...], coef[...].reshape(NB * BLK, BLK), preferred_element_type=F32)
        for o in range(4):
            out[:, o * BLK : (o + 1) * BLK] = acc[o * T : (o + 1) * T].astype(BF16)

    def permute_t(val):
        return jnp.dot(val, perm[...], preferred_element_type=F32)

    def layer_half(l, rows_ref, agg, sum_ref, br, r):
        def norm(i, _):
            rows = pl.ds(pl.multiple_of(r * 256 + i * BLK, BLK), BLK)
            up = lax.dot_general(
                agg[:, rows], wup[l], (((0,), (0,)), ((), ())), preferred_element_type=F32
            )
            s = rows_ref[rows, :].astype(F32) + up
            if sum_ref is not None:
                sum_ref[rows, :] = s
            scale = lax.rsqrt(jnp.mean(s * s, axis=-1, keepdims=True) + 1e-06)
            nrm[rows, :] = (gain_ref[l : l + 1, :] * s * scale).astype(BF16)
            return 0

        for i in range(2):
            norm(i, 0)
        rows = pl.ds(r * 256 if isinstance(r, int) else pl.multiple_of(r * 256, 256), 256)
        h = jnp.dot(nrm[rows, :], win[l], preferred_element_type=F32)
        h = 0.5 * h
        act[rows, :] = (h + h * jnp.tanh(h)).astype(BF16)
        val = jnp.dot(act[rows, :], wout[l], preferred_element_type=F32).astype(BF16)
        if br is None:
            out_ref[rows, :] = (
                (summed[rows, :] + branch[rows, :].astype(F32)) + val.astype(F32)
            ).astype(BF16)
        else:
            br[rows, :] = val

    def layer(l, rows_ref, agg, sum_ref, br):
        for r in (0, 1):
            layer_half(l, rows_ref, agg, sum_ref, br, r)

    def by_rows(f):
        def body(r, _):
            f(pl.ds(pl.multiple_of(r * BLK, BLK), BLK))
            return 0

        lax.fori_loop(0, 4, body, 0)

    for j in range(SUB):
        leg1_start(j)

    for i in range(8, 12):
        loads[i].wait()

    def onehot(rows, r):
        ids = lax.broadcasted_iota(jnp.int32, (BLK, E), 0) + r * BLK
        perm[rows, :] = jnp.where(ids == rs_ref[0:1, :], 1.0, 0.0).astype(BF16)

    def onehot_body(r, _):
        onehot(pl.ds(pl.multiple_of(r * BLK, BLK), BLK), r)
        return 0

    lax.fori_loop(0, 4, onehot_body, 0)

    _, z_step, y_step, finish, drain0 = gat0
    z_step(1)
    leg2_own(0)
    leg2_own(1)
    y_step(0)
    leg1_wait(0)
    leg2_start(0)
    leg2_own(2)
    leg2_own(3)
    z_step(2)
    leg1_wait(1)
    leg2_start(1)
    y_step(1)
    leg1_wait(2)
    leg2_start(2)
    leg2_own(4)
    leg2_own(5)
    leg1_wait(3)
    leg2_start(3)
    z_step(3)
    leg2_own(6)
    leg2_own(7)
    z_step(4)
    leg1_wait(4)
    leg2_start(4)
    y_step(2)
    leg2_relay(0)
    leg1_wait(5)
    leg2_start(5)
    y_step(3)
    leg1_wait(6)
    leg2_start(6)
    leg2_relay(2)
    leg1_wait(7)
    leg2_start(7)
    y_step(4)
    finish()
    loads[2].wait()
    triplets(g0, aggt.at[0])
    swap_start(0, aggt.at[0], aggm.at[0])
    leg2_relay(4)
    for i in (3, 4, 5):
        loads[i].wait()
    for r in (0, 1):
        rows = pl.ds(r * 256, 256)
        layer_half(0, st, aggt.at[0], summed, branch, r)
        pbt[r] = proj_t(1, branch[rows, :]).astype(BF16)
        swap_start(1 + r, pbt.at[r], pbm.at[r])
        if r == 0:
            leg2_wait(1)
            leg3_start(1)
            leg2_wait(3)
            leg3_start(3)

    def part_sum(rows):
        nrm[rows, :] = (summed[rows, :] + branch[rows, :].astype(F32)).astype(BF16)

    by_rows(part_sum)
    half1 = proj_t(1, nrm[...])
    leg2_relay(6)
    leg2_wait(5)
    leg3_start(5)
    leg2_wait(7)
    leg3_start(7)
    swap_wait(1, pbt.at[0], pbm.at[0])
    swap_wait(2, pbt.at[1], pbm.at[1])
    mirrored_pb = jnp.dot(pbm[0], perm[0:256, :], preferred_element_type=F32) + jnp.dot(
        pbm[1], perm[256:512, :], preferred_element_type=F32
    )
    put_own(g1, half1 + mirrored_pb)
    start, z_step, y_step, finish, drain1 = gat1
    start()
    z_step(1)
    y_step(0)
    z_step(2)
    y_step(1)
    swap_wait(0, aggt.at[0], aggm.at[0])
    act[0:T, 0:E] = permute_t(aggm[0]).astype(BF16)
    aggm[0] = act[0:T, 0:E]
    z_step(3)
    z_step(4)
    y_step(2)
    for j in range(SUB):
        leg3_wait(j)

    def take_rows(r, _):
        rows = pl.ds(pl.multiple_of(r * 256, 256), 256)
        mst[rows, :] = lax.dot_general(
            perm[:, rows], fin[...], (((0,), (0,)), ((), ())), preferred_element_type=F32
        ).astype(BF16)
        return 0

    lax.fori_loop(0, 2, take_rows, 0)
    layer_half(0, mst, aggm.at[0], msum, mbr, 0)
    y_step(3)
    y_step(4)
    finish()
    triplets(g1, aggt.at[1])
    swap_start(3, aggt.at[1], aggm.at[1])
    layer_half(0, mst, aggm.at[0], msum, mbr, 1)

    def next_state(rows):
        b = branch[rows, :].astype(F32)
        m = mbr[rows, :].astype(F32)
        st[rows, :] = ((summed[rows, :] + b) + m).astype(BF16)
        mst[rows, :] = ((msum[rows, :] + m) + b).astype(BF16)

    legs_drain()
    by_rows(next_state)

    for i in (6, 7):
        loads[i].wait()
    layer(1, st, aggt.at[1], summed, branch)
    swap_wait(3, aggt.at[1], aggm.at[1])
    act[0:T, 0:E] = permute_t(aggm[1]).astype(BF16)
    aggm[1] = act[0:T, 0:E]
    layer(1, mst, aggm.at[1], None, None)

    drain0()
    drain1()
    swap_drain(0, aggt.at[0], aggm.at[0])
    swap_drain(1, pbt.at[0], pbm.at[0])
    swap_drain(2, pbt.at[1], pbm.at[1])
    swap_drain(3, aggt.at[1], aggm.at[1])


def local(
    edge_states, triplet_coeff, block_target, block_source, block_count, reverse_slot,
    w_proj, w_up, w_in, w_out, norm_gain,
):
    vmem = pl.BlockSpec(memory_space=pltpu.VMEM)
    smem = pl.BlockSpec(memory_space=pltpu.SMEM)
    hbm = pl.BlockSpec(memory_space=pltpu.HBM)
    dma = pltpu.SemaphoreType.DMA
    def stay(a):
        return pltpu.with_memory_space_constraint(a, pltpu.HBM)

    out = pl.pallas_call(
        kernel,
        out_shape=jax.ShapeDtypeStruct((E, D), BF16),
        in_specs=[hbm, hbm, smem] + [hbm] * 8,
        out_specs=vmem,
        scratch_shapes=[
            pltpu.SMEM((NB,), jnp.int32),
            pltpu.SMEM((NB,), jnp.int32),
            pltpu.VMEM((1, E), jnp.int32),
            pltpu.VMEM((2, D), F32),
            pltpu.VMEM((E, D), BF16),
            pltpu.VMEM((NB, BLK, BLK), BF16),
            pltpu.VMEM((2, T, D), BF16),
            pltpu.VMEM((2, T, D), BF16),
            pltpu.VMEM((2, D, D), BF16),
            pltpu.VMEM((2, D, D), BF16),
            pltpu.VMEM((NBLK, T, BLK), BF16),
            pltpu.VMEM((NBLK, T, BLK), BF16),
            pltpu.VMEM((4, BLK, D), BF16),
            pltpu.VMEM((4, BLK, D), BF16),
            pltpu.VMEM((SUB // 2, 8, ROWS, D), BF16),
            pltpu.VMEM((E, D), BF16),
            pltpu.VMEM((E, E), BF16),
            pltpu.VMEM((4 * T, NB * BLK), BF16),
            pltpu.VMEM((2, T, E), BF16),
            pltpu.VMEM((2, T, E), BF16),
            pltpu.VMEM((2, T, 256), BF16),
            pltpu.VMEM((2, T, 256), BF16),
            pltpu.VMEM((E, D), F32),
            pltpu.VMEM((E, D), BF16),
            pltpu.VMEM((E, D), BF16),
            pltpu.VMEM((E, D), F32),
            pltpu.VMEM((E, D), BF16),
            pltpu.VMEM((E, D), BF16),
            pltpu.VMEM((E, D), BF16),
            dma((12,)),
            dma((2,)),
            dma((2, 9, 2)),
            dma((2, 2, 4, 2)),
            dma((2,)),
            dma((SUB,)), dma((SUB, 4)),
            dma((SUB,)), dma((SUB, 4)),
            dma((SUB // 2,)), dma((SUB // 2, 8)),
            dma((SUB,)), dma((SUB, 4)),
            dma((4,)), dma((4,)),
        ],
        compiler_params=pltpu.CompilerParams(
            collective_id=0, has_side_effects=True, vmem_limit_bytes=48 << 20
        ),
        name="edge_layers",
    )(
        *map(stay, (block_target[0, 0], block_source[0, 0])),
        block_count[0],
        *map(
            stay,
            (
                reverse_slot[0], norm_gain, edge_states[0, 0], triplet_coeff[0, 0],
                jnp.swapaxes(w_proj, 1, 2), w_up, w_in, w_out,
            ),
        ),
    )
    return out[None, None]


def solution(mesh):
    return jax.shard_map(
        local,
        mesh=mesh,
        in_specs=(
            P("src", "tgt", None, None),
            P("src", "tgt", None, None, None),
            P("src", "tgt", None),
            P("src", "tgt", None),
            P("src", "tgt"),
            P("src", "tgt", None),
            P(),
            P(),
            P(),
            P(),
            P(),
        ),
        out_specs=P("src", "tgt", None, None),
        check_vma=False,
    )
```
